32 devices in a mesh: ctx: 8 (over y, x, core), ch: 4 (over z).
Axes of the slice: x: 2, y: 2, z: 4, core: 2. Of those that a mesh axis runs over, the one named last changes fastest.
Arguments:
- tokens_in: bfloat16 [1792, 4096], P('ctx', 'ch'), may hold values from -6 to 6
- norm_gain: bfloat16 [4096], P('ch'), may hold values from 0.5 to 1.5
- w_qkv: bfloat16 [4096, 3, 2048], P('ch'), may hold values from -0.09375 to 0.09375
- short_filter: float32 [3, 3, 2048], P(None, None, 'ch'), may hold values from -3.5 to 3.5
- residue: float32 [2048, 16], P('ch'), may hold values from -1.5 to 1.5
- decay_rate: float32 [2048, 16], P('ch'), may hold values from 0.00027901787 to 0.025
- skip_bias: float32 [2048], P('ch'), may hold values from -4 to 4
- w_out: bfloat16 [2048, 4096], P(None, 'ch'), may hold values from -0.125 to 0.125
Outputs:
- mixed_out: bfloat16 [1792, 4096], P('ctx', 'ch')
The draws below stay inside these ranges and needn't reach their ends.
All inputs are finite; a program needn't handle non-finite values.
Results may differ from the reference program's by a relative error of at most 0.011.
Values may be sent and summed in bfloat16 or wider, within the bound.
A program may use at most 128 MiB of HBM per device.

```python
import math
import jax
import jax.numpy as jnp
from jax import lax

D = 4096
SHORT = 3
ORDER = 16
TOKENS = 1792
SLAB = 2048


def level_of(own_key, dims, cuts, smallest, largest):
    loudness = 1.0
    for dim, shards_of in cuts:
        heights = jax.random.uniform(jax.random.fold_in(jax.random.fold_in(own_key, 6), dim), (shards_of,), jnp.float32, smallest / len(cuts), largest / len(cuts))
        loudness = loudness * jnp.repeat(jnp.exp(heights), dims[dim] // shards_of).reshape((-1,) + (1,) * (len(dims) - 1 - dim))
    return loudness


def normal_values(stream_key, dims, scale, most, split=(), dtype=jnp.bfloat16):
    result = scale * jax.random.normal(stream_key, dims, jnp.float32)
    if split:
        result = result * level_of(stream_key, dims, split, -0.22, 0.18)
    return jnp.clip(result, -most, most).astype(dtype)


def setup_inputs(seed: int = 0) -> dict:
    key_list = jax.random.split(jax.random.key(seed), 9)
    return {
        "tokens_in": normal_values(key_list[0], (TOKENS, D), 1.0, 6.0, ((0, 8), (1, 4))),
        "norm_gain": jnp.clip(1.0 + 0.1 * jax.random.normal(key_list[1], (D,), jnp.float32), 0.5, 1.5).astype(jnp.bfloat16),
        "w_qkv": normal_values(key_list[2], (D, 3, SLAB), D ** -0.5, 0.09375, ((0, 4),)),
        "short_filter": normal_values(key_list[3], (SHORT, 3, SLAB), SHORT ** -0.5, 3.5, ((2, 4),), jnp.float32),
        "residue": normal_values(key_list[4], (SLAB, ORDER), ORDER ** -0.5, 1.5, ((0, 4),), jnp.float32),
        "decay_rate": jnp.clip(jnp.exp(math.log(0.025) - 4.495355 * jax.random.uniform(key_list[5], (SLAB, ORDER), jnp.float32) ** level_of(key_list[5], (SLAB, ORDER), ((0, 4),), -0.2, 0.2)), 0.00027901787, 0.025),
        "skip_bias": normal_values(key_list[6], (SLAB,), 1.0, 4.0, ((0, 4),), jnp.float32),
        "w_out": normal_values(key_list[7], (SLAB, D), SLAB ** -0.5, 0.125, ((1, 4),)),
    }


def reference(tokens_in, norm_gain, w_qkv, short_filter, residue, decay_rate, skip_bias, w_out):
    total = tokens_in.shape[0]
    chans = w_qkv.shape[2]
    wide = tokens_in.astype(jnp.float32)
    scaled = (wide * norm_gain.astype(jnp.float32)).astype(jnp.bfloat16)
    mean_sq = lax.optimization_barrier(jnp.mean(wide * wide, axis=1))
    proj = jnp.dot(scaled, w_qkv.reshape(D, 3 * chans), preferred_element_type=jnp.float32).reshape(total, 3, chans)
    feats = (proj * lax.rsqrt(mean_sq + 1e-06)[:, None, None]).astype(jnp.bfloat16)
    padded = jnp.concatenate([jnp.zeros((SHORT - 1, 3, chans), jnp.bfloat16), feats], axis=0).astype(jnp.float32)
    featurized = sum((short_filter[lag_index][None] * padded[SHORT - 1 - lag_index:SHORT - 1 - lag_index + total] for lag_index in range(SHORT)))
    query = featurized[:, 0]
    gated = (featurized[:, 1] * featurized[:, 2]).astype(jnp.bfloat16)
    lag_values = lax.iota(jnp.float32, total)
    block_size = 32
    blocks = chans // block_size
    signal = gated.astype(jnp.float32).T.reshape(blocks, block_size, total)
    residues = residue.reshape(blocks, block_size, ORDER)
    decays = decay_rate.reshape(blocks, block_size, ORDER)

    def block_conv(packed):
        block_signal, block_residue, block_decay = packed
        filt = lax.optimization_barrier(jnp.sum(block_residue[:, :, None] * jnp.sqrt(2.0 * block_decay)[:, :, None] * jnp.exp(-block_decay[:, :, None] * lag_values[None, None, :]), axis=1))
        spectrum = jnp.fft.rfft(block_signal, n=2 * total) * jnp.fft.rfft(filt, n=2 * total)
        return jnp.fft.irfft(spectrum, n=2 * total)[:, :total]
    conv = lax.map(block_conv, (signal, residues, decays)).reshape(chans, total).T.astype(jnp.bfloat16)
    gated_out = (query * (conv.astype(jnp.float32) + skip_bias[None, :] * gated.astype(jnp.float32))).astype(jnp.bfloat16)
    return jnp.dot(gated_out, w_out, preferred_element_type=jnp.float32).astype(jnp.bfloat16)
```

```python
import functools

import jax
import jax.numpy as jnp
from jax import lax
from jax.experimental import pallas as pl
from jax.experimental.pallas import tpu as pltpu
from jax.sharding import PartitionSpec as P

D = 4096
SHORT = 3
ORDER = 16
LANES = 128
SUB = 32
HALO = 16
MESH = pl.DeviceIdType.MESH


def sum_pieces(rows):
    cut = rows // 2 // 16 * 16
    return ((0, cut), (cut, rows - cut))


def gated_pieces(rows):
    cut = -(-rows // 2 // SUB) * SUB
    return ((0, cut), (cut, rows - cut))


def kernel(
    n_ctx, n_ch, rows, chunks,
    tok_hbm, gain_ref, w_hbm, sf_ref, res_ref, dec_ref, skip_ref, wout_hbm, out_ref,
    tok, scaled, wbuf, woutbuf, a_send, a_recv, b_send, b_recv, n_send, n_recv,
    sq_send, sq_recv, square, scale_ref, p_sf, p_res, p_dec, p_skip,
    fpad, halo_send, halo_recv, st_send, st_recv, local_st, gz, gated_ref, query_ref, local_y, gobuf, acc,
    tok_sem, w_sem, wout_sem, a_ss, a_rs, b_ss, b_rs, n_ss, n_rs, sq_ss, sq_rs, p_ss, p_rs,
    h_ss, h_rs, st_ss, st_rs, g_ss, g_rs, own_ss,
):
    me = lax.axis_index("ctx")
    z = lax.axis_index("ch")
    last = n_ch - 1
    own = chunks - 1
    per = sf_ref.shape[2] // LANES
    blocks = rows // SUB
    sum_cuts = sum_pieces(rows)
    gated_cuts = gated_pieces(rows)
    is_end = (z == 0) | (z == last)
    is_mid = (z > 0) & (z < last)
    near = jnp.where(z * 2 > last, 1, 0)
    step_out = 1 - 2 * near
    outward = jnp.clip(z + step_out, 0, last)
    inward = jnp.clip(z - step_out, 0, last)

    def slot(half, i):
        return jnp.where(half == 0, i, 2 * chunks - 1 - i)

    def near_slot(i):
        return slot(near, i)

    def far_slot(i):
        return slot(1 - near, i)

    barrier = pltpu.get_barrier_semaphore()
    for k in range(1, n_ch):
        pl.semaphore_signal(
            barrier, inc=1, device_id={"ch": lax.rem(z + k, n_ch)}, device_id_type=MESH
        )

    def greet(k, _):
        pl.semaphore_signal(
            barrier, inc=1, device_id={"ctx": lax.rem(me + k, n_ctx)}, device_id_type=MESH
        )
        return 0

    lax.fori_loop(1, n_ctx, greet, 0)

    def weight_copy(g):
        return pltpu.make_async_copy(
            w_hbm.at[:, :, pl.ds(pl.multiple_of(g * LANES, LANES), LANES)], wbuf.at[g], w_sem.at[g]
        )

    tok_copy = pltpu.make_async_copy(tok_hbm, tok, tok_sem)
    tok_copy.start()
    weight_copy(far_slot(0)).start()
    weight_copy(near_slot(0)).start()

    def start_weights(j, _):
        weight_copy(far_slot(j)).start()
        weight_copy(near_slot(j)).start()
        return 0

    lax.fori_loop(1, chunks, start_weights, 0)
    wout_copy = pltpu.make_async_copy(wout_hbm, woutbuf, wout_sem)
    wout_copy.start()

    tok_copy.wait()
    wide = tok[...].astype(jnp.float32)
    scaled[...] = (wide * gain_ref[...].astype(jnp.float32).reshape(1, -1)).astype(jnp.bfloat16)

    def partial(g):
        weight_copy(g).wait()
        taps = jnp.concatenate([wbuf[g, s] for s in range(3)], axis=1)
        return jnp.dot(scaled[...], taps, preferred_element_type=jnp.float32)

    def a_copy(j, i):
        first, size = sum_cuts[i]
        return pltpu.make_async_remote_copy(
            src_ref=a_send.at[j, pl.ds(first, size)], dst_ref=a_recv.at[j, pl.ds(first, size)],
            send_sem=a_ss.at[j, i], recv_sem=a_rs.at[j, i],
            device_id={"ch": outward}, device_id_type=MESH,
        )

    def ab_copy(j, i):
        first, size = sum_cuts[i]
        return pltpu.make_async_remote_copy(
            src_ref=a_send.at[j, pl.ds(first, size)], dst_ref=b_recv.at[j, pl.ds(first, size)],
            send_sem=a_ss.at[j, i], recv_sem=b_rs.at[j, i],
            device_id={"ch": outward}, device_id_type=MESH,
        )

    def b_copy(j, i):
        first, size = sum_cuts[i]
        return pltpu.make_async_remote_copy(
            src_ref=b_send.at[j, pl.ds(first, size)], dst_ref=b_recv.at[j, pl.ds(first, size)],
            send_sem=b_ss.at[j, i], recv_sem=b_rs.at[j, i],
            device_id={"ch": inward}, device_id_type=MESH,
        )

    n_copy = pltpu.make_async_remote_copy(
        src_ref=n_send, dst_ref=n_recv, send_sem=n_ss, recv_sem=n_rs,
        device_id={"ch": outward}, device_id_type=MESH,
    )

    def sq_copy(k):
        return pltpu.make_async_remote_copy(
            src_ref=sq_send, dst_ref=sq_recv.at[k - 1], send_sem=sq_ss.at[k - 1],
            recv_sem=sq_rs.at[k - 1], device_id={"ch": lax.rem(z + k, n_ch)}, device_id_type=MESH,
        )

    p_copies = [
        pltpu.make_async_remote_copy(
            src_ref=src, dst_ref=dst.at[1], send_sem=p_ss.at[i], recv_sem=p_rs.at[i],
            device_id={"ch": inward}, device_id_type=MESH,
        )
        for i, (src, dst) in enumerate(
            ((sf_ref, p_sf), (res_ref, p_res), (dec_ref, p_dec), (skip_ref, p_skip))
        )
    ]

    def halo_copy(j):
        return pltpu.make_async_remote_copy(
            src_ref=halo_send.at[j], dst_ref=halo_recv.at[j], send_sem=h_ss.at[j],
            recv_sem=h_rs.at[j], device_id={"ctx": jnp.minimum(me + 1, n_ctx - 1)}, device_id_type=MESH,
        )

    def state_copy(j, k):
        return pltpu.make_async_remote_copy(
            src_ref=st_send.at[j], dst_ref=st_recv.at[j, k - 1], send_sem=st_ss.at[j],
            recv_sem=st_rs.at[j], device_id={"ctx": lax.rem(me + k, n_ctx)}, device_id_type=MESH,
        )

    def g_copy(g, i, target):
        first, size = gated_cuts[i]
        piece = gobuf.at[g, pl.ds(first, size)]
        return pltpu.make_async_remote_copy(
            src_ref=piece, dst_ref=piece, send_sem=g_ss.at[g, i], recv_sem=g_rs.at[g, i],
            device_id={"ch": target}, device_id_type=MESH,
        )

    def own_copy(i):
        first, size = gated_cuts[i]
        piece = gobuf.at[near_slot(own), pl.ds(first, size)]
        return pltpu.make_async_remote_copy(
            src_ref=piece, dst_ref=piece, send_sem=own_ss.at[i], recv_sem=g_rs.at[near_slot(own), i],
            device_id={"ch": inward}, device_id_type=MESH,
        )

    first_far = partial(far_slot(0))
    a_send[0] = first_far.astype(jnp.bfloat16)
    pl.semaphore_wait(barrier, n_ch - 1 + n_ctx - 1)

    @pl.when(is_end)
    def _():
        for i in range(len(sum_cuts)):
            a_copy(0, i).start()
        p_sf[0] = sf_ref[...]
        p_res[0] = res_ref[...]
        p_dec[0] = dec_ref[...]
        p_skip[0] = skip_ref[...]

    @pl.when(is_mid)
    def _():
        for copy in p_copies:
            copy.start()
        p_sf[1] = sf_ref[...]
        p_res[1] = res_ref[...]
        p_dec[1] = dec_ref[...]
        p_skip[1] = skip_ref[...]

    again = tok[...].astype(jnp.float32)
    again = again * again
    folded = again[:, :LANES]
    for k in range(1, again.shape[1] // LANES):
        folded = folded + again[:, k * LANES : (k + 1) * LANES]
    square[...] = jnp.zeros_like(square)
    square[pl.ds(0, rows), :] = folded
    sq_send[...] = jnp.sum(square[...].T, axis=0, keepdims=True)
    for k in range(1, n_ch):
        sq_copy(k).start()
    gz[...] = jnp.zeros_like(gz)

    def finish_scale():
        for k in range(1, n_ch):
            sq_copy(k).wait_recv()
        total = sq_send[...]
        for k in range(1, n_ch):
            total = total + sq_recv[k - 1]
        mean_sq = jnp.broadcast_to(total * (1.0 / D), (LANES, total.shape[1])).T
        scale_ref[...] = lax.rsqrt(mean_sq + 1e-06)[:rows]

    def stage_a(j, proj):
        scale = scale_ref[...]
        for s in range(3):
            feats = (proj[:, s * LANES : (s + 1) * LANES] * scale).astype(jnp.bfloat16)
            fpad[j, s, pl.ds(HALO, rows), :] = feats.astype(jnp.float32)
            halo_send[j, s] = feats[rows - HALO :]

        @pl.when(me < n_ctx - 1)
        def _():
            halo_copy(j).start()

    def lane_of(j):
        place = lax.rem(j, per)
        place = jnp.where(near == 0, place, per - 1 - place)
        return j // per, pl.ds(pl.multiple_of(place * LANES, LANES), LANES)

    def stage_b(j):
        side, lanes = lane_of(j)

        @pl.when(me > 0)
        def _():
            halo_copy(j).wait_recv()
            for s in range(3):
                fpad[j, s, pl.ds(0, HALO), :] = halo_recv[j, s].astype(jnp.float32)

        @pl.when(me == 0)
        def _():
            for s in range(3):
                fpad[j, s, pl.ds(0, HALO), :] = jnp.zeros((HALO, LANES), jnp.float32)

        def featurized(s):
            total = p_sf[side, 0, pl.ds(s, 1), lanes] * fpad[j, s, pl.ds(HALO, rows), :]
            for lag in range(1, SHORT):
                tap = p_sf[side, lag, pl.ds(s, 1), lanes]
                total = total + tap * fpad[j, s, pl.ds(HALO - lag, rows), :]
            return total

        query_ref[j] = featurized(0)
        gated = (featurized(1) * featurized(2)).astype(jnp.bfloat16).astype(jnp.float32)
        gated_ref[j] = gated
        for b in range(blocks):
            gz[b, pl.ds(SUB, SUB), :] = gated[b * SUB : (b + 1) * SUB]
        decay = p_dec[side, :, lanes]
        weight = p_res[side, :, lanes] * jnp.sqrt(2.0 * decay)
        lag_rows = lax.broadcasted_iota(jnp.int32, (SUB, LANES), 0).astype(jnp.float32)
        taps = jnp.zeros((SUB, LANES), jnp.float32)
        for r in range(ORDER):
            taps = taps + weight[r : r + 1] * jnp.exp(-decay[r : r + 1] * lag_rows)
        falls = [jnp.exp(decay * (-float(SUB - 1 - u))) for u in range(SUB)]
        jump = jnp.exp(decay * (-float(SUB)))

        def block(b, state):
            local_st[j, b] = state
            total = taps[0:1] * gz[b, pl.ds(SUB, SUB), :]
            for k in range(1, SUB):
                total = total + taps[k : k + 1] * gz[b, pl.ds(SUB - k, SUB), :]
            local_y[j, b] = total
            state = state * jump
            for u in range(SUB):
                state = state + falls[u] * gz[b, pl.ds(SUB + u, 1), :]
            return state

        state = lax.fori_loop(0, blocks, block, jnp.zeros((ORDER, LANES), jnp.float32))
        st_send[j] = state

        def send(k, _):
            state_copy(j, k).start()
            return 0

        lax.fori_loop(1, n_ctx, send, 0)

    def stage_c(j):
        side, lanes = lane_of(j)
        pltpu.make_async_copy(st_recv.at[j], st_recv.at[j], st_rs.at[j]).wait()
        decay = p_dec[side, :, lanes]
        weight = p_res[side, :, lanes] * jnp.sqrt(2.0 * decay)

        def gather(k, state):
            far = jnp.full((ORDER, LANES), (k - 1) * rows, jnp.int32).astype(jnp.float32)
            term = jnp.exp(-decay * far) * st_recv[j, k - 1]
            return state + jnp.where(jnp.full((ORDER, LANES), k, jnp.int32) <= me, term, 0.0)

        incoming = lax.fori_loop(1, n_ctx, gather, jnp.zeros((ORDER, LANES), jnp.float32))
        lag_rows = lax.broadcasted_iota(jnp.int32, (SUB, LANES), 0).astype(jnp.float32) + 1.0
        tables = [
            weight[r : r + 1] * jnp.exp(-decay[r : r + 1] * lag_rows) for r in range(ORDER)
        ]
        jump = jnp.exp(decay * (-float(SUB)))
        skip = p_skip[side, :, lanes]
        g = near_slot(j)
        done = 0
        for b in range(blocks):
            state = local_st[j, b] + incoming
            total = local_y[j, b]
            for r in range(ORDER):
                total = total + tables[r] * state[r : r + 1]
            conv = total.astype(jnp.bfloat16).astype(jnp.float32)
            span = pl.ds(b * SUB, SUB)
            mixed = query_ref[j, span, :] * (conv + skip * gated_ref[j, span, :])
            gobuf[g, span, :] = mixed.astype(jnp.bfloat16)
            incoming = incoming * jump
            if (b + 1) * SUB == sum(gated_cuts[done]):
                i = done
                g_copy(g, i, outward).start()

                @pl.when(is_mid)
                def _():
                    own_copy(i).start()

                done += 1

    tile = 256
    width_out = out_ref.shape[1]

    def project(p, how):
        lhs = jnp.concatenate([gobuf[2 * p], gobuf[2 * p + 1]], axis=1)

        def column(t, _):
            cols = pl.ds(pl.multiple_of(t * tile, tile), tile)
            rhs = woutbuf[pl.ds(pl.multiple_of(p * 2 * LANES, 2 * LANES), 2 * LANES), cols]
            part = jnp.dot(lhs, rhs, preferred_element_type=jnp.float32)
            if how == "first":
                acc[:, cols] = part
            elif how == "more":
                acc[:, cols] += part
            else:
                out_ref[:, cols] = (acc[:, cols] + part).astype(jnp.bfloat16)
            return 0

        lax.fori_loop(0, width_out // tile, column, 0)

    def pair_of(half, i):
        return jnp.where(half == 0, i, chunks - 1 - i)

    def recv_gated(g):
        for i in range(len(gated_cuts)):
            g_copy(g, i, outward).wait_recv()

    def relay(g, target):
        for i in range(len(gated_cuts)):
            g_copy(g, i, target).wait_recv()
            g_copy(g, i, target).start()

    @pl.when(is_end)
    def _():
        def lead(j, _):
            a_send[j] = partial(far_slot(j)).astype(jnp.bfloat16)
            for i in range(len(sum_cuts)):
                a_copy(j, i).start()
            return 0

        lax.fori_loop(1, chunks, lead, 0)
        n_send[...] = partial(near_slot(own)).astype(jnp.bfloat16)
        n_copy.start()
        finish_scale()
        for copy in p_copies:
            copy.wait_recv()

        def step(s, _):
            @pl.when(s < own)
            def _():
                total = partial(near_slot(s))
                for i in range(len(sum_cuts)):
                    b_copy(s, i).wait_recv()
                stage_a(s, total + b_recv[s].astype(jnp.float32))

            @pl.when((s >= 1) & (s < own + 1))
            def _():
                stage_b(s - 1)

            @pl.when(s >= 2)
            def _():
                stage_c(s - 2)

            return 0

        lax.fori_loop(0, own + 2, step, 0)
        wout_copy.wait()
        pairs = chunks // 2
        project(pair_of(near, 0), "first")

        def near_pairs(k, _):
            project(pair_of(near, k), "more")
            return 0

        lax.fori_loop(1, pairs - 1, near_pairs, 0)

        def far_pairs(k, _):
            recv_gated(far_slot(2 * k))
            recv_gated(far_slot(2 * k + 1))
            project(pair_of(1 - near, k), "more")
            return 0

        lax.fori_loop(0, pairs - 1, far_pairs, 0)
        recv_gated(near_slot(own))
        project(pair_of(near, pairs - 1), "more")
        recv_gated(far_slot(own))
        recv_gated(far_slot(own - 1))
        project(pair_of(1 - near, pairs - 1), "last")

    @pl.when(is_mid)
    def _():
        def pass_out(s, total):
            for i, (first, size) in enumerate(sum_cuts):
                span = pl.ds(first, size)
                a_copy(s, i).wait_recv()
                theirs = a_recv[s, span, :].astype(jnp.float32)
                a_send[s, span, :] = (total[first : first + size] + theirs).astype(jnp.bfloat16)
                ab_copy(s, i).start()

        def step(s, _):
            total = partial(near_slot(s))
            for i, (first, size) in enumerate(sum_cuts):
                span = pl.ds(first, size)
                b_copy(s, i).wait_recv()
                theirs = b_recv[s, span, :].astype(jnp.float32)
                b_send[s, span, :] = (total[first : first + size] + theirs).astype(jnp.bfloat16)
                b_copy(s, i).start()

            @pl.when(s + 2 < chunks)
            def _():
                pass_out(s + 2, partial(far_slot(s + 2)))

            return 0

        pass_out(0, first_far)
        pass_out(1, partial(far_slot(1)))
        lax.fori_loop(0, own, step, 0)

        finish_scale()
        total = partial(near_slot(own))
        for i in range(len(sum_cuts)):
            b_copy(own, i).wait_recv()
        n_copy.wait_recv()
        stage_a(own, total + b_recv[own].astype(jnp.float32) + n_recv[...].astype(jnp.float32))
        relay(near_slot(0), outward)
        stage_b(own)
        relay(near_slot(1), outward)
        relay(near_slot(2), outward)
        stage_c(own)
        relay(near_slot(3), outward)
        relay(far_slot(0), inward)
        relay(near_slot(4), outward)
        relay(far_slot(1), inward)
        relay(near_slot(5), outward)
        relay(far_slot(2), inward)
        relay(near_slot(6), outward)
        relay(far_slot(own), inward)
        relay(far_slot(3), inward)
        relay(far_slot(4), inward)
        relay(far_slot(5), inward)
        wout_copy.wait()
        pairs = chunks // 2
        project(pair_of(near, 0), "first")

        def near_pairs(k, _):
            project(pair_of(near, k), "more")
            return 0

        lax.fori_loop(1, pairs, near_pairs, 0)

        def far_pairs(k, _):
            project(pair_of(1 - near, k), "more")
            return 0

        lax.fori_loop(0, pairs - 1, far_pairs, 0)
        relay(far_slot(6), inward)
        project(pair_of(1 - near, pairs - 1), "last")

    def drain(j, _):
        for i in range(len(sum_cuts)):
            a_copy(j, i).wait_send()

        @pl.when(is_mid & (j < own))
        def _():
            for i in range(len(sum_cuts)):
                b_copy(j, i).wait_send()

        @pl.when(is_end & (j < own))
        def _():
            for i in range(len(gated_cuts)):
                g_copy(near_slot(j), i, outward).wait_send()

        @pl.when(is_mid)
        def _():
            for i in range(len(gated_cuts)):
                g_copy(near_slot(j), i, outward).wait_send()
                g_copy(far_slot(j), i, inward).wait_send()

        mine = jnp.where(is_end, jnp.where(j < own, 1, 0), jnp.where(j == own, 1, 0))

        @pl.when((mine == 1) & (me < n_ctx - 1))
        def _():
            halo_copy(j).wait_send()

        @pl.when(mine == 1)
        def _():
            pltpu.make_async_copy(st_recv.at[j], st_recv.at[j], st_ss.at[j]).wait()

        return 0

    lax.fori_loop(0, chunks, drain, 0)
    for k in range(1, n_ch):
        sq_copy(k).wait_send()

    @pl.when(is_end)
    def _():
        n_copy.wait_send()

    @pl.when(is_mid)
    def _():
        for copy in p_copies:
            copy.wait_send()
        for i in range(len(gated_cuts)):
            own_copy(i).wait_send()


def local(tokens_in, norm_gain, w_qkv, short_filter, residue, decay_rate, skip_bias, w_out):
    rows, feat = tokens_in.shape
    slab = w_qkv.shape[2]
    dev_ch = short_filter.shape[2]
    n_ctx = lax.axis_size("ctx")
    n_ch = lax.axis_size("ch")
    chunks = slab // 2 // LANES
    width = 3 * LANES
    padded = -(-rows // LANES) * LANES
    blocks = rows // SUB
    vmem = pl.BlockSpec(memory_space=pltpu.VMEM)
    hbm = pl.BlockSpec(memory_space=pl.ANY)
    bf, f32 = jnp.bfloat16, jnp.float32
    dma = pltpu.SemaphoreType.DMA
    V = pltpu.VMEM
    n_sum = len(sum_pieces(rows))
    n_gated = len(gated_pieces(rows))
    return pl.pallas_call(
        functools.partial(kernel, n_ctx, n_ch, rows, chunks),
        out_shape=jax.ShapeDtypeStruct((rows, w_out.shape[1]), bf),
        in_specs=[hbm, vmem, hbm, vmem, vmem, vmem, vmem, hbm],
        out_specs=vmem,
        scratch_shapes=[
            V((rows, feat), bf), V((rows, feat), bf), V((2 * chunks, 3, feat, LANES), bf), V(w_out.shape, bf),
            V((chunks, rows, width), bf), V((chunks, rows, width), bf),
            V((chunks, rows, width), bf), V((chunks, rows, width), bf),
            V((rows, width), bf), V((rows, width), bf),
            V((1, padded), f32), V((n_ch - 1, 1, padded), f32), V((padded, LANES), f32),
            V((rows, LANES), f32),
            V((2, SHORT, 3, dev_ch), f32), V((2, ORDER, dev_ch), f32), V((2, ORDER, dev_ch), f32),
            V((2, 1, dev_ch), f32),
            V((chunks, 3, HALO + rows, LANES), f32),
            V((chunks, 3, HALO, LANES), bf), V((chunks, 3, HALO, LANES), bf),
            V((chunks, ORDER, LANES), f32), V((chunks, n_ctx - 1, ORDER, LANES), f32),
            V((chunks, blocks, ORDER, LANES), f32), V((blocks, 2 * SUB, LANES), f32),
            V((chunks, rows, LANES), f32), V((chunks, rows, LANES), f32),
            V((chunks, blocks, SUB, LANES), f32), V((2 * chunks, rows, LANES), bf),
            V((rows, w_out.shape[1]), f32),
            dma, dma((2 * chunks,)), dma, dma((chunks, n_sum)), dma((chunks, n_sum)),
            dma((chunks, n_sum)), dma((chunks, n_sum)), dma, dma,
            dma((n_ch - 1,)), dma((n_ch - 1,)), dma((4,)), dma((4,)),
            dma((chunks,)), dma((chunks,)), dma((chunks,)), dma((chunks,)),
            dma((2 * chunks, n_gated)), dma((2 * chunks, n_gated)), dma((n_gated,)),
        ],
        compiler_params=pltpu.CompilerParams(
            collective_id=0, has_side_effects=True, vmem_limit_bytes=58 * 2**20
        ),
        name="hyena",
    )(
        tokens_in, norm_gain, jnp.transpose(w_qkv, (1, 0, 2)), short_filter,
        residue.T, decay_rate.T, skip_bias.reshape(1, dev_ch), w_out,
    )


def solution(mesh):
    return jax.shard_map(
        local,
        mesh=mesh,
        in_specs=(
            P("ctx", "ch"),
            P("ch"),
            P("ch", None, None),
            P(None, None, "ch"),
            P("ch", None),
            P("ch", None),
            P("ch"),
            P(None, "ch"),
        ),
        out_specs=P("ctx", "ch"),
        check_vma=False,
    )
```

```python
import functools

import jax
import jax.numpy as jnp
from jax import lax
from jax.experimental import pallas as pl
from jax.experimental.pallas import tpu as pltpu
from jax.sharding import PartitionSpec as P

D = 4096
SHORT = 3
ORDER = 16
LANES = 128
SUB = 32
HALO = 16
MESH = pl.DeviceIdType.MESH


def sum_pieces(rows):
    cut = rows // 2 // 16 * 16
    return ((0, cut), (cut, rows - cut))


def gated_pieces(rows):
    cut = -(-rows // 2 // SUB) * SUB
    return ((0, cut), (cut, rows - cut))


def kernel(
    n_ctx, n_ch, rows, chunks,
    tok_hbm, gain_hbm, w_hbm, sf_hbm, res_hbm, dec_hbm, skip_hbm, wout_hbm, out_ref,
    tok, gain, scaled, wbuf, woutbuf, a_send, a_recv, b_send, b_recv, n_send, n_recv,
    sq_send, sq_recv, sq_own, square, scale_ref, p_sf, p_res, p_dec, p_skip,
    fpad, halo_send, halo_recv, st_send, st_recv, local_st, gz, gated_ref, query_ref, local_y, gobuf, acc,
    tok_sem, gain_sem, l_sem, w_sem, wout_sem, rounds, a_ss, a_rs, b_ss, b_rs, n_ss, n_rs, sq_ss, sq_rs, p_ss, p_rs,
    h_ss, h_rs, st_ss, st_rs, g_ss, g_rs, own_ss,
):
    me = lax.axis_index("ctx")
    z = lax.axis_index("ch")
    last = n_ch - 1
    own = chunks - 1
    per = sf_hbm.shape[2] // LANES
    depth = n_ctx.bit_length() - 1
    assert 1 << depth == n_ctx
    blocks = rows // SUB
    sum_cuts = sum_pieces(rows)
    gated_cuts = gated_pieces(rows)
    is_end = (z == 0) | (z == last)
    is_mid = (z > 0) & (z < last)
    near = jnp.where(z * 2 > last, 1, 0)
    step_out = 1 - 2 * near
    outward = jnp.clip(z + step_out, 0, last)
    inward = jnp.clip(z - step_out, 0, last)

    def slot(half, i):
        return jnp.where(half == 0, i, 2 * chunks - 1 - i)

    def near_slot(i):
        return slot(near, i)

    def far_slot(i):
        return slot(1 - near, i)

    def peer(k):
        bit = lax.rem(me // (1 << k), 2)
        return me + (1 << k) * (1 - 2 * bit)

    barrier = pltpu.get_barrier_semaphore()
    pl.semaphore_signal(barrier, inc=1, device_id={"ch": outward}, device_id_type=MESH)

    @pl.when(is_mid)
    def _():
        pl.semaphore_signal(barrier, inc=1, device_id={"ch": inward}, device_id_type=MESH)

    for k in range(depth):
        pl.semaphore_signal(barrier, inc=1, device_id={"ctx": peer(k)}, device_id_type=MESH)

    def call_round(k):
        pl.semaphore_signal(rounds.at[k], inc=1, device_id={"ctx": peer(k)}, device_id_type=MESH)

    def next_round(k):
        pl.semaphore_wait(rounds.at[k], 1)
        if k + 1 < depth:
            call_round(k + 1)

    def weight_copy(g):
        return pltpu.make_async_copy(
            w_hbm.at[:, :, pl.ds(pl.multiple_of(g * LANES, LANES), LANES)], wbuf.at[g], w_sem.at[g]
        )

    tok_copy = pltpu.make_async_copy(tok_hbm, tok, tok_sem)
    tok_copy.start()
    gain_copy = pltpu.make_async_copy(gain_hbm, gain, gain_sem)
    gain_copy.start()
    weight_copy(far_slot(0)).start()
    weight_copy(near_slot(0)).start()

    def start_weights(j, _):
        weight_copy(far_slot(j)).start()
        weight_copy(near_slot(j)).start()
        return 0

    lax.fori_loop(1, chunks, start_weights, 0)
    wout_copy = pltpu.make_async_copy(wout_hbm, woutbuf, wout_sem)
    wout_copy.start()
    home = jnp.where(is_end, 0, 1)
    l_copies = [
        pltpu.make_async_copy(src, dst.at[home], l_sem.at[i])
        for i, (src, dst) in enumerate(
            ((sf_hbm, p_sf), (res_hbm, p_res), (dec_hbm, p_dec), (skip_hbm, p_skip))
        )
    ]
    for copy in l_copies:
        copy.start()

    tok_copy.wait()
    gain_copy.wait()
    wide = tok[...].astype(jnp.float32)
    scaled[...] = (wide * gain[...].astype(jnp.float32).reshape(1, -1)).astype(jnp.bfloat16)

    def partial(g):
        weight_copy(g).wait()
        taps = jnp.concatenate([wbuf[g, s] for s in range(3)], axis=1)
        return jnp.dot(scaled[...], taps, preferred_element_type=jnp.float32)

    def a_copy(j, i):
        first, size = sum_cuts[i]
        return pltpu.make_async_remote_copy(
            src_ref=a_send.at[j, pl.ds(first, size)], dst_ref=a_recv.at[j, pl.ds(first, size)],
            send_sem=a_ss.at[j, i], recv_sem=a_rs.at[j, i],
            device_id={"ch": outward}, device_id_type=MESH,
        )

    def ab_copy(j, i):
        first, size = sum_cuts[i]
        return pltpu.make_async_remote_copy(
            src_ref=a_send.at[j, pl.ds(first, size)], dst_ref=b_recv.at[j, pl.ds(first, size)],
            send_sem=a_ss.at[j, i], recv_sem=b_rs.at[j, i],
            device_id={"ch": outward}, device_id_type=MESH,
        )

    def b_copy(j, i):
        first, size = sum_cuts[i]
        return pltpu.make_async_remote_copy(
            src_ref=b_send.at[j, pl.ds(first, size)], dst_ref=b_recv.at[j, pl.ds(first, size)],
            send_sem=b_ss.at[j, i], recv_sem=b_rs.at[j, i],
            device_id={"ch": inward}, device_id_type=MESH,
        )

    n_copy = pltpu.make_async_remote_copy(
        src_ref=n_send, dst_ref=n_recv, send_sem=n_ss, recv_sem=n_rs,
        device_id={"ch": outward}, device_id_type=MESH,
    )

    def sq_copy(way, target):
        return pltpu.make_async_remote_copy(
            src_ref=sq_send.at[way], dst_ref=sq_recv.at[way], send_sem=sq_ss.at[way],
            recv_sem=sq_rs.at[way], device_id={"ch": target}, device_id_type=MESH,
        )

    p_copies = [
        pltpu.make_async_remote_copy(
            src_ref=dst.at[1], dst_ref=dst.at[1], send_sem=p_ss.at[i], recv_sem=p_rs.at[i],
            device_id={"ch": inward}, device_id_type=MESH,
        )
        for i, dst in enumerate((p_sf, p_res, p_dec, p_skip))
    ]

    def halo_copy(j):
        return pltpu.make_async_remote_copy(
            src_ref=halo_send.at[j], dst_ref=halo_recv.at[j], send_sem=h_ss.at[j],
            recv_sem=h_rs.at[j], device_id={"ctx": jnp.minimum(me + 1, n_ctx - 1)}, device_id_type=MESH,
        )

    def state_copy(j, k):
        return pltpu.make_async_remote_copy(
            src_ref=st_send.at[j], dst_ref=st_recv.at[j, k - 1], send_sem=st_ss.at[j],
            recv_sem=st_rs.at[j], device_id={"ctx": lax.rem(me + k, n_ctx)}, device_id_type=MESH,
        )

    def g_copy(g, i, target):
        first, size = gated_cuts[i]
        piece = gobuf.at[g, pl.ds(first, size)]
        return pltpu.make_async_remote_copy(
            src_ref=piece, dst_ref=piece, send_sem=g_ss.at[g, i], recv_sem=g_rs.at[g, i],
            device_id={"ch": target}, device_id_type=MESH,
        )

    def own_copy(i):
        first, size = gated_cuts[i]
        piece = gobuf.at[near_slot(own), pl.ds(first, size)]
        return pltpu.make_async_remote_copy(
            src_ref=piece, dst_ref=piece, send_sem=own_ss.at[i], recv_sem=g_rs.at[near_slot(own), i],
            device_id={"ch": inward}, device_id_type=MESH,
        )

    first_far = partial(far_slot(0))
    a_send[0] = first_far.astype(jnp.bfloat16)

    @pl.when(is_end)
    def _():
        pl.semaphore_wait(barrier, 1 + depth)
        a_copy(0, 0).start()

    @pl.when(is_mid)
    def _():
        pl.semaphore_wait(barrier, 2 + depth)

    call_round(0)
    again = tok[...].astype(jnp.float32)
    again = again * again
    folded = again[:, :LANES]
    for k in range(1, again.shape[1] // LANES):
        folded = folded + again[:, k * LANES : (k + 1) * LANES]
    square[...] = jnp.zeros_like(square)
    square[pl.ds(0, rows), :] = folded
    sq_own[...] = jnp.sum(square[...].T, axis=0, keepdims=True)

    @pl.when(is_end)
    def _():
        sq_send[0] = sq_own[...]
        sq_copy(0, outward).start()
        for i in range(1, len(sum_cuts)):
            a_copy(0, i).start()

    def await_own():
        for copy in l_copies:
            copy.wait()

    gz[...] = jnp.zeros_like(gz)
    acc[...] = jnp.zeros_like(acc)

    def set_scale(total):
        mean_sq = jnp.broadcast_to(total * (1.0 / D), (LANES, total.shape[1])).T
        scale_ref[...] = lax.rsqrt(mean_sq + 1e-06)[:rows]

    def stage_a(j, proj):
        scale = scale_ref[...]
        for s in range(3):
            feats = (proj[:, s * LANES : (s + 1) * LANES] * scale).astype(jnp.bfloat16)
            fpad[j, s, pl.ds(HALO, rows), :] = feats.astype(jnp.float32)
            halo_send[j, s] = feats[rows - HALO :]

        @pl.when(me < n_ctx - 1)
        def _():
            halo_copy(j).start()

    def lane_of(j):
        place = lax.rem(j, per)
        place = jnp.where(near == 0, place, per - 1 - place)
        return j // per, pl.ds(pl.multiple_of(place * LANES, LANES), LANES)

    def stage_b(j):
        side, lanes = lane_of(j)

        @pl.when(me > 0)
        def _():
            halo_copy(j).wait_recv()
            for s in range(3):
                fpad[j, s, pl.ds(0, HALO), :] = halo_recv[j, s].astype(jnp.float32)

        @pl.when(me == 0)
        def _():
            for s in range(3):
                fpad[j, s, pl.ds(0, HALO), :] = jnp.zeros((HALO, LANES), jnp.float32)

        def featurized(s):
            total = p_sf[side, 0, pl.ds(s, 1), lanes] * fpad[j, s, pl.ds(HALO, rows), :]
            for lag in range(1, SHORT):
                tap = p_sf[side, lag, pl.ds(s, 1), lanes]
                total = total + tap * fpad[j, s, pl.ds(HALO - lag, rows), :]
            return total

        query_ref[j] = featurized(0)
        gated = (featurized(1) * featurized(2)).astype(jnp.bfloat16).astype(jnp.float32)
        gated_ref[j] = gated
        for b in range(blocks):
            gz[b, pl.ds(SUB, SUB), :] = gated[b * SUB : (b + 1) * SUB]
        decay = p_dec[side, :, lanes]
        weight = p_res[side, :, lanes] * jnp.sqrt(2.0 * decay)
        lag_rows = lax.broadcasted_iota(jnp.int32, (SUB, LANES), 0).astype(jnp.float32)
        taps = jnp.zeros((SUB, LANES), jnp.float32)
        for r in range(ORDER):
            taps = taps + weight[r : r + 1] * jnp.exp(-decay[r : r + 1] * lag_rows)
        falls = [jnp.exp(decay * (-float(SUB - 1 - u))) for u in range(SUB)]
        jump = jnp.exp(decay * (-float(SUB)))

        def block(b, state):
            local_st[j, b] = state
            total = taps[0:1] * gz[b, pl.ds(SUB, SUB), :]
            for k in range(1, SUB):
                total = total + taps[k : k + 1] * gz[b, pl.ds(SUB - k, SUB), :]
            local_y[j, b] = total
            state = state * jump
            for u in range(SUB):
                state = state + falls[u] * gz[b, pl.ds(SUB + u, 1), :]
            return state

        state = lax.fori_loop(0, blocks, block, jnp.zeros((ORDER, LANES), jnp.float32))
        st_send[j] = state

        def send(k, _):
            state_copy(j, k).start()
            return 0

        lax.fori_loop(1, n_ctx, send, 0)

    def stage_c(j):
        side, lanes = lane_of(j)
        pltpu.make_async_copy(st_recv.at[j], st_recv.at[j], st_rs.at[j]).wait()
        decay = p_dec[side, :, lanes]
        weight = p_res[side, :, lanes] * jnp.sqrt(2.0 * decay)

        def gather(k, state):
            far = jnp.full((ORDER, LANES), (k - 1) * rows, jnp.int32).astype(jnp.float32)
            term = jnp.exp(-decay * far) * st_recv[j, k - 1]
            return state + jnp.where(jnp.full((ORDER, LANES), k, jnp.int32) <= me, term, 0.0)

        incoming = lax.fori_loop(1, n_ctx, gather, jnp.zeros((ORDER, LANES), jnp.float32))
        lag_rows = lax.broadcasted_iota(jnp.int32, (SUB, LANES), 0).astype(jnp.float32) + 1.0
        tables = [
            weight[r : r + 1] * jnp.exp(-decay[r : r + 1] * lag_rows) for r in range(ORDER)
        ]
        jump = jnp.exp(decay * (-float(SUB)))
        skip = p_skip[side, :, lanes]
        g = near_slot(j)
        done = 0
        for b in range(blocks):
            state = local_st[j, b] + incoming
            total = local_y[j, b]
            for r in range(ORDER):
                total = total + tables[r] * state[r : r + 1]
            conv = total.astype(jnp.bfloat16).astype(jnp.float32)
            span = pl.ds(b * SUB, SUB)
            mixed = query_ref[j, span, :] * (conv + skip * gated_ref[j, span, :])
            gobuf[g, span, :] = mixed.astype(jnp.bfloat16)
            incoming = incoming * jump
            if (b + 1) * SUB == sum(gated_cuts[done]):
                i = done
                g_copy(g, i, outward).start()

                @pl.when(is_mid)
                def _():
                    own_copy(i).start()

                done += 1

    tile = 256
    width_out = out_ref.shape[1]

    def project(p, final=False):
        lhs = jnp.concatenate([gobuf[2 * p], gobuf[2 * p + 1]], axis=1)

        def column(t, _):
            cols = pl.ds(pl.multiple_of(t * tile, tile), tile)
            rhs = woutbuf[pl.ds(pl.multiple_of(p * 2 * LANES, 2 * LANES), 2 * LANES), cols]
            part = jnp.dot(lhs, rhs, preferred_element_type=jnp.float32)
            if final:
                out_ref[:, cols] = (acc[:, cols] + part).astype(jnp.bfloat16)
            else:
                acc[:, cols] += part
            return 0

        lax.fori_loop(0, width_out // tile, column, 0)

    def pair_of(half, i):
        return jnp.where(half == 0, i, chunks - 1 - i)

    def recv_gated(g):
        for i in range(len(gated_cuts)):
            g_copy(g, i, outward).wait_recv()

    def relay(g, target):
        for i in range(len(gated_cuts)):
            g_copy(g, i, target).wait_recv()
            g_copy(g, i, target).start()

    @pl.when(is_end)
    def _():
        def lead(j, _):
            a_send[j] = partial(far_slot(j)).astype(jnp.bfloat16)
            for i in range(len(sum_cuts)):
                a_copy(j, i).start()
            return 0

        lax.fori_loop(1, chunks, lead, 0)
        n_send[...] = partial(near_slot(own)).astype(jnp.bfloat16)
        n_copy.start()
        for k in range(depth):
            next_round(k)
        await_own()
        for copy in p_copies:
            copy.wait_recv()
        sq_copy(2, outward).wait_recv()
        set_scale(sq_own[...] + sq_recv[2])
        wout_copy.wait()

        def step(s, _):
            @pl.when(s < own)
            def _():
                total = partial(near_slot(s))
                for i in range(len(sum_cuts)):
                    b_copy(s, i).wait_recv()
                stage_a(s, total + b_recv[s].astype(jnp.float32))

            @pl.when((s >= 1) & (s < own + 1))
            def _():
                stage_b(s - 1)

            @pl.when(s >= 2)
            def _():
                stage_c(s - 2)

            @pl.when((s >= 3) & (lax.rem(s, 2) == 1))
            def _():
                project(pair_of(near, (s - 3) // 2))

            return 0

        lax.fori_loop(0, own + 2, step, 0)
        pairs = chunks // 2

        def far_pairs(k, _):
            recv_gated(far_slot(2 * k))
            recv_gated(far_slot(2 * k + 1))
            project(pair_of(1 - near, k))
            return 0

        lax.fori_loop(0, pairs - 2, far_pairs, 0)
        recv_gated(near_slot(own))
        project(pair_of(near, pairs - 1))
        far_pairs(pairs - 2, 0)
        recv_gated(far_slot(own))
        recv_gated(far_slot(own - 1))
        project(pair_of(1 - near, pairs - 1), True)

    @pl.when(is_mid)
    def _():
        def pass_out(s, total):
            for i, (first, size) in enumerate(sum_cuts):
                span = pl.ds(first, size)
                a_copy(s, i).wait_recv()
                theirs = a_recv[s, span, :].astype(jnp.float32)
                a_send[s, span, :] = (total[first : first + size] + theirs).astype(jnp.bfloat16)
                ab_copy(s, i).start()

        def step(s, _):
            total = partial(near_slot(s))
            for i, (first, size) in enumerate(sum_cuts):
                span = pl.ds(first, size)
                b_copy(s, i).wait_recv()
                theirs = b_recv[s, span, :].astype(jnp.float32)
                b_send[s, span, :] = (total[first : first + size] + theirs).astype(jnp.bfloat16)
                b_copy(s, i).start()

            @pl.when(s + 2 < chunks)
            def _():
                pass_out(s + 2, partial(far_slot(s + 2)))

            return 0

        await_own()
        for copy in p_copies:
            copy.start()
        pass_out(0, first_far)
        sq_copy(0, outward).wait_recv()
        sq_send[1] = sq_own[...] + sq_recv[0]
        sq_copy(1, outward).start()
        next_round(0)
        pass_out(1, partial(far_slot(1)))
        sq_copy(1, outward).wait_recv()
        sq_send[2] = sq_own[...] + sq_recv[1]
        sq_copy(2, inward).start()
        set_scale(sq_own[...] + sq_recv[0] + sq_recv[1])
        next_round(1)
        lax.fori_loop(0, own, step, 0)
        for k in range(2, depth):
            next_round(k)
        total = partial(near_slot(own))
        for i in range(len(sum_cuts)):
            b_copy(own, i).wait_recv()
        n_copy.wait_recv()
        stage_a(own, total + b_recv[own].astype(jnp.float32) + n_recv[...].astype(jnp.float32))
        wout_copy.wait()

        def out(i):
            relay(near_slot(i), outward)

        def back(i):
            relay(far_slot(i), inward)

        out(0)
        stage_b(own)
        out(1)
        back(0)
        out(2)
        project(pair_of(near, 0))
        back(1)
        out(3)
        back(2)
        stage_c(own)
        out(4)
        back(3)
        project(pair_of(near, 1))
        out(5)
        back(own)
        project(pair_of(1 - near, 0))
        out(6)
        back(4)
        back(5)
        project(pair_of(near, 2))
        back(6)
        project(pair_of(near, 3))
        project(pair_of(1 - near, 1))
        project(pair_of(1 - near, 2))
        project(pair_of(1 - near, 3), True)

    def drain(j, _):
        for i in range(len(sum_cuts)):
            a_copy(j, i).wait_send()

        @pl.when(is_mid & (j < own))
        def _():
            for i in range(len(sum_cuts)):
                b_copy(j, i).wait_send()

        @pl.when(is_end & (j < own))
        def _():
            for i in range(len(gated_cuts)):
                g_copy(near_slot(j), i, outward).wait_send()

        @pl.when(is_mid)
        def _():
            for i in range(len(gated_cuts)):
                g_copy(near_slot(j), i, outward).wait_send()
                g_copy(far_slot(j), i, inward).wait_send()

        mine = jnp.where(is_end, jnp.where(j < own, 1, 0), jnp.where(j == own, 1, 0))

        @pl.when((mine == 1) & (me < n_ctx - 1))
        def _():
            halo_copy(j).wait_send()

        @pl.when(mine == 1)
        def _():
            pltpu.make_async_copy(st_recv.at[j], st_recv.at[j], st_ss.at[j]).wait()

        return 0

    lax.fori_loop(0, chunks, drain, 0)
    @pl.when(is_end)
    def _():
        n_copy.wait_send()
        sq_copy(0, outward).wait_send()

    @pl.when(is_mid)
    def _():
        for copy in p_copies:
            copy.wait_send()
        sq_copy(1, outward).wait_send()
        sq_copy(2, inward).wait_send()
        for i in range(len(gated_cuts)):
            own_copy(i).wait_send()


def local(tokens_in, norm_gain, w_qkv, short_filter, residue, decay_rate, skip_bias, w_out):
    rows, feat = tokens_in.shape
    slab = w_qkv.shape[2]
    dev_ch = short_filter.shape[2]
    n_ctx = lax.axis_size("ctx")
    n_ch = lax.axis_size("ch")
    chunks = slab // 2 // LANES
    width = 3 * LANES
    padded = -(-rows // LANES) * LANES
    blocks = rows // SUB
    vmem = pl.BlockSpec(memory_space=pltpu.VMEM)
    hbm = pl.BlockSpec(memory_space=pl.ANY)
    bf, f32 = jnp.bfloat16, jnp.float32
    dma = pltpu.SemaphoreType.DMA
    V = pltpu.VMEM
    n_sum = len(sum_pieces(rows))
    n_gated = len(gated_pieces(rows))
    return pl.pallas_call(
        functools.partial(kernel, n_ctx, n_ch, rows, chunks),
        out_shape=pltpu.VMEM((rows, w_out.shape[1]), bf),
        in_specs=[hbm] * 8,
        out_specs=vmem,
        scratch_shapes=[
            V((rows, feat), bf), V((feat,), bf), V((rows, feat), bf), V((2 * chunks, 3, feat, LANES), bf), V(w_out.shape, bf),
            V((chunks, rows, width), bf), V((chunks, rows, width), bf),
            V((chunks, rows, width), bf), V((chunks, rows, width), bf),
            V((rows, width), bf), V((rows, width), bf),
            V((3, 1, padded), f32), V((3, 1, padded), f32), V((1, padded), f32), V((padded, LANES), f32),
            V((rows, LANES), f32),
            V((2, SHORT, 3, dev_ch), f32), V((2, ORDER, dev_ch), f32), V((2, ORDER, dev_ch), f32),
            V((2, 1, dev_ch), f32),
            V((chunks, 3, HALO + rows, LANES), f32),
            V((chunks, 3, HALO, LANES), bf), V((chunks, 3, HALO, LANES), bf),
            V((chunks, ORDER, LANES), f32), V((chunks, n_ctx - 1, ORDER, LANES), f32),
            V((chunks, blocks, ORDER, LANES), f32), V((blocks, 2 * SUB, LANES), f32),
            V((chunks, rows, LANES), f32), V((chunks, rows, LANES), f32),
            V((chunks, blocks, SUB, LANES), f32), V((2 * chunks, rows, LANES), bf),
            V((rows, w_out.shape[1]), f32),
            dma, dma, dma((4,)), dma((2 * chunks,)), dma, pltpu.SemaphoreType.REGULAR((n_ctx.bit_length() - 1,)),
            dma((chunks, n_sum)), dma((chunks, n_sum)),
            dma((chunks, n_sum)), dma((chunks, n_sum)), dma, dma,
            dma((3,)), dma((3,)), dma((4,)), dma((4,)),
            dma((chunks,)), dma((chunks,)), dma((chunks,)), dma((chunks,)),
            dma((2 * chunks, n_gated)), dma((2 * chunks, n_gated)), dma((n_gated,)),
        ],
        compiler_params=pltpu.CompilerParams(
            collective_id=0, has_side_effects=True, vmem_limit_bytes=58 * 2**20
        ),
        name="hyena",
    )(
        tokens_in, norm_gain, jnp.transpose(w_qkv, (1, 0, 2)), short_filter,
        residue.T, decay_rate.T, skip_bias.reshape(1, dev_ch), w_out,
    )


def solution(mesh):
    return jax.shard_map(
        local,
        mesh=mesh,
        in_specs=(
            P("ctx", "ch"),
            P("ch"),
            P("ch", None, None),
            P(None, None, "ch"),
            P("ch", None),
            P("ch", None),
            P("ch"),
            P(None, "ch"),
        ),
        out_specs=P("ctx", "ch"),
        check_vma=False,
    )
```

```python
import functools

import jax
import jax.numpy as jnp
from jax import lax
from jax.experimental import pallas as pl
from jax.experimental.pallas import tpu as pltpu
from jax.sharding import PartitionSpec as P

D = 4096
SHORT = 3
ORDER = 16
LANES = 128
SUB = 32
HALO = 16
N_AFTER = (2, 2)
MESH = pl.DeviceIdType.MESH


def sum_pieces(rows):
    cut = rows // 2 // 16 * 16
    return ((0, cut), (cut, rows - cut))


def gated_pieces(rows):
    cut = -(-rows // 2 // SUB) * SUB
    return ((0, cut), (cut, rows - cut))


def kernel(
    n_ctx, n_ch, rows, chunks,
    tok_hbm, gain_hbm, w_hbm, sf_hbm, res_hbm, dec_hbm, skip_hbm, wout_hbm, out_ref,
    tok, gain, scaled, wbuf, woutbuf, a_send, a_recv, b_send, b_recv, n_send, n_recv,
    sq_send, sq_recv, sq_own, square, scale_ref, p_sf, p_res, p_dec, p_skip,
    fpad, halo_send, halo_recv, st_send, st_recv, local_st, gz, gated_ref, query_ref, local_y, gobuf, acc,
    tok_sem, gain_sem, l_sem, w_sem, wout_sem, rounds, a_ss, a_rs, b_ss, b_rs, n_ss, n_rs, sq_ss, sq_rs, p_ss, p_rs,
    h_ss, h_rs, st_ss, st_rs, g_ss, g_rs, own_ss,
):
    me = lax.axis_index("ctx")
    z = lax.axis_index("ch")
    last = n_ch - 1
    own = chunks - 1
    per = sf_hbm.shape[2] // LANES
    depth = n_ctx.bit_length() - 1
    assert 1 << depth == n_ctx
    blocks = rows // SUB
    sum_cuts = sum_pieces(rows)
    gated_cuts = gated_pieces(rows)
    is_end = (z == 0) | (z == last)
    is_mid = (z > 0) & (z < last)
    near = jnp.where(z * 2 > last, 1, 0)
    step_out = 1 - 2 * near
    outward = jnp.clip(z + step_out, 0, last)
    inward = jnp.clip(z - step_out, 0, last)

    def slot(half, i):
        return jnp.where(half == 0, i, 2 * chunks - 1 - i)

    def near_slot(i):
        return slot(near, i)

    def far_slot(i):
        return slot(1 - near, i)

    def weight_copy(g):
        return pltpu.make_async_copy(
            w_hbm.at[:, :, pl.ds(pl.multiple_of(g * LANES, LANES), LANES)], wbuf.at[g], w_sem.at[g]
        )

    tok_copy = pltpu.make_async_copy(tok_hbm, tok, tok_sem)
    tok_copy.start()
    gain_copy = pltpu.make_async_copy(gain_hbm, gain, gain_sem)
    gain_copy.start()
    weight_copy(far_slot(0)).start()

    def peer(k):
        bit = lax.rem(me // (1 << k), 2)
        return me + (1 << k) * (1 - 2 * bit)

    barrier = pltpu.get_barrier_semaphore()
    pl.semaphore_signal(barrier, inc=1, device_id={"ch": outward}, device_id_type=MESH)

    @pl.when(is_mid)
    def _():
        pl.semaphore_signal(barrier, inc=1, device_id={"ch": inward}, device_id_type=MESH)

    for k in range(depth):
        pl.semaphore_signal(barrier, inc=1, device_id={"ctx": peer(k)}, device_id_type=MESH)

    def call_round(k):
        pl.semaphore_signal(rounds.at[k], inc=1, device_id={"ctx": peer(k)}, device_id_type=MESH)

    def next_round(k):
        pl.semaphore_wait(rounds.at[k], 1)
        if k + 1 < depth:
            call_round(k + 1)

    wout_copy = pltpu.make_async_copy(wout_hbm, woutbuf, wout_sem)
    home = jnp.where(is_end, 0, 1)
    l_copies = [
        pltpu.make_async_copy(src, dst.at[home], l_sem.at[i])
        for i, (src, dst) in enumerate(
            ((sf_hbm, p_sf), (res_hbm, p_res), (dec_hbm, p_dec), (skip_hbm, p_skip))
        )
    ]
    tok_copy.wait()
    gain_copy.wait()
    wide = tok[...].astype(jnp.float32)
    scaled[...] = (wide * gain[...].astype(jnp.float32).reshape(1, -1)).astype(jnp.bfloat16)

    def partial(g):
        weight_copy(g).wait()
        taps = jnp.concatenate([wbuf[g, s] for s in range(3)], axis=1)
        return jnp.dot(scaled[...], taps, preferred_element_type=jnp.float32)

    def a_copy(j, i):
        first, size = sum_cuts[i]
        return pltpu.make_async_remote_copy(
            src_ref=a_send.at[j, pl.ds(first, size)], dst_ref=a_recv.at[j, pl.ds(first, size)],
            send_sem=a_ss.at[j, i], recv_sem=a_rs.at[j, i],
            device_id={"ch": outward}, device_id_type=MESH,
        )

    def ab_copy(j, i):
        first, size = sum_cuts[i]
        return pltpu.make_async_remote_copy(
            src_ref=a_send.at[j, pl.ds(first, size)], dst_ref=b_recv.at[j, pl.ds(first, size)],
            send_sem=a_ss.at[j, i], recv_sem=b_rs.at[j, i],
            device_id={"ch": outward}, device_id_type=MESH,
        )

    def b_copy(j, i):
        first, size = sum_cuts[i]
        return pltpu.make_async_remote_copy(
            src_ref=b_send.at[j, pl.ds(first, size)], dst_ref=b_recv.at[j, pl.ds(first, size)],
            send_sem=b_ss.at[j, i], recv_sem=b_rs.at[j, i],
            device_id={"ch": inward}, device_id_type=MESH,
        )

    def n_copy(i):
        first, size = sum_cuts[i]
        return pltpu.make_async_remote_copy(
            src_ref=n_send.at[pl.ds(first, size)], dst_ref=n_recv.at[pl.ds(first, size)],
            send_sem=n_ss.at[i], recv_sem=n_rs.at[i],
            device_id={"ch": outward}, device_id_type=MESH,
        )

    def sq_copy(way, target):
        return pltpu.make_async_remote_copy(
            src_ref=sq_send.at[way], dst_ref=sq_recv.at[way], send_sem=sq_ss.at[way],
            recv_sem=sq_rs.at[way], device_id={"ch": target}, device_id_type=MESH,
        )

    p_copies = [
        pltpu.make_async_remote_copy(
            src_ref=dst.at[1], dst_ref=dst.at[1], send_sem=p_ss.at[i], recv_sem=p_rs.at[i],
            device_id={"ch": inward}, device_id_type=MESH,
        )
        for i, dst in enumerate((p_sf, p_res, p_dec, p_skip))
    ]

    def halo_copy(j):
        return pltpu.make_async_remote_copy(
            src_ref=halo_send.at[j], dst_ref=halo_recv.at[j], send_sem=h_ss.at[j],
            recv_sem=h_rs.at[j], device_id={"ctx": jnp.minimum(me + 1, n_ctx - 1)}, device_id_type=MESH,
        )

    def state_copy(j, k):
        return pltpu.make_async_remote_copy(
            src_ref=st_send.at[j], dst_ref=st_recv.at[j, k - 1], send_sem=st_ss.at[j],
            recv_sem=st_rs.at[j], device_id={"ctx": lax.rem(me + k, n_ctx)}, device_id_type=MESH,
        )

    def g_copy(g, i, target):
        first, size = gated_cuts[i]
        piece = gobuf.at[g, pl.ds(first, size)]
        return pltpu.make_async_remote_copy(
            src_ref=piece, dst_ref=piece, send_sem=g_ss.at[g, i], recv_sem=g_rs.at[g, i],
            device_id={"ch": target}, device_id_type=MESH,
        )

    def far_end_copy(g, i):
        first, size = gated_cuts[i]
        piece = gobuf.at[g, pl.ds(first, size)]
        return pltpu.make_async_remote_copy(
            src_ref=piece, dst_ref=piece, send_sem=own_ss.at[i], recv_sem=g_rs.at[g, i],
            device_id={"ch": last - z}, device_id_type=MESH,
        )

    def own_copy(i):
        first, size = gated_cuts[i]
        piece = gobuf.at[near_slot(own), pl.ds(first, size)]
        return pltpu.make_async_remote_copy(
            src_ref=piece, dst_ref=piece, send_sem=own_ss.at[i], recv_sem=g_rs.at[near_slot(own), i],
            device_id={"ch": inward}, device_id_type=MESH,
        )

    first_far = partial(far_slot(0))
    a_send[0] = first_far.astype(jnp.bfloat16)

    @pl.when(is_end)
    def _():
        pl.semaphore_wait(barrier, 1 + depth)
        a_copy(0, 0).start()

    @pl.when(is_mid)
    def _():
        pl.semaphore_wait(barrier, 2 + depth)

    call_round(0)
    for copy in l_copies:
        copy.start()
    weight_copy(near_slot(0)).start()

    def start_weights(j, _):
        weight_copy(far_slot(j)).start()
        weight_copy(near_slot(j)).start()
        return 0

    lax.fori_loop(1, chunks, start_weights, 0)
    wout_copy.start()
    again = tok[...].astype(jnp.float32)
    again = again * again
    folded = again[:, :LANES]
    for k in range(1, again.shape[1] // LANES):
        folded = folded + again[:, k * LANES : (k + 1) * LANES]
    square[...] = jnp.zeros_like(square)
    square[pl.ds(0, rows), :] = folded
    sq_own[...] = jnp.sum(square[...].T, axis=0, keepdims=True)

    @pl.when(is_end)
    def _():
        sq_send[0] = sq_own[...]
        sq_copy(0, outward).start()
        for i in range(1, len(sum_cuts)):
            a_copy(0, i).start()

    def await_own():
        for copy in l_copies:
            copy.wait()

    gz[...] = jnp.zeros_like(gz)
    acc[...] = jnp.zeros_like(acc)

    def set_scale(total):
        mean_sq = jnp.broadcast_to(total * (1.0 / D), (LANES, total.shape[1])).T
        scale_ref[...] = lax.rsqrt(mean_sq + 1e-06)[:rows]

    def stage_a(j, proj):
        scale = scale_ref[...]
        for s in range(3):
            tail = proj[rows - HALO :, s * LANES : (s + 1) * LANES] * scale[rows - HALO :]
            halo_send[j, s] = tail.astype(jnp.bfloat16)

        @pl.when(me < n_ctx - 1)
        def _():
            halo_copy(j).start()

        for s in range(3):
            feats = (proj[:, s * LANES : (s + 1) * LANES] * scale).astype(jnp.bfloat16)
            fpad[j, s, pl.ds(HALO, rows), :] = feats.astype(jnp.float32)

    def lane_of(j):
        place = lax.rem(j, per)
        place = jnp.where(near == 0, place, per - 1 - place)
        return j // per, pl.ds(pl.multiple_of(place * LANES, LANES), LANES)

    def stage_b(j):
        side, lanes = lane_of(j)
        decay = p_dec[side, :, lanes]
        weight = p_res[side, :, lanes] * jnp.sqrt(2.0 * decay)
        lag_rows = lax.broadcasted_iota(jnp.int32, (SUB, LANES), 0).astype(jnp.float32)
        taps = jnp.zeros((SUB, LANES), jnp.float32)
        for r in range(ORDER):
            taps = taps + weight[r : r + 1] * jnp.exp(-decay[r : r + 1] * lag_rows)
        falls = [jnp.exp(decay * (-float(SUB - 1 - u))) for u in range(SUB)]
        jump = jnp.exp(decay * (-float(SUB)))

        @pl.when(me > 0)
        def _():
            halo_copy(j).wait_recv()
            for s in range(3):
                fpad[j, s, pl.ds(0, HALO), :] = halo_recv[j, s].astype(jnp.float32)

        @pl.when(me == 0)
        def _():
            for s in range(3):
                fpad[j, s, pl.ds(0, HALO), :] = jnp.zeros((HALO, LANES), jnp.float32)

        def featurized(s):
            total = p_sf[side, 0, pl.ds(s, 1), lanes] * fpad[j, s, pl.ds(HALO, rows), :]
            for lag in range(1, SHORT):
                tap = p_sf[side, lag, pl.ds(s, 1), lanes]
                total = total + tap * fpad[j, s, pl.ds(HALO - lag, rows), :]
            return total

        gated = (featurized(1) * featurized(2)).astype(jnp.bfloat16).astype(jnp.float32)
        gated_ref[j] = gated
        for b in range(blocks):
            gz[b, pl.ds(SUB, SUB), :] = gated[b * SUB : (b + 1) * SUB]

        def block(b, state):
            local_st[j, b] = state
            parts = [state * jump] + [None] * 3
            for u in range(SUB):
                term = falls[u] * gz[b, pl.ds(SUB + u, 1), :]
                way = (u + 1) % 4
                parts[way] = term if parts[way] is None else parts[way] + term
            return (parts[0] + parts[1]) + (parts[2] + parts[3])

        state = lax.fori_loop(0, blocks, block, jnp.zeros((ORDER, LANES), jnp.float32))
        st_send[j] = state

        if n_ctx <= 8:
            for k in range(1, n_ctx):
                state_copy(j, k).start()
        else:
            lax.fori_loop(1, n_ctx, lambda k, _: (state_copy(j, k).start(), 0)[1], 0)

        query_ref[j] = featurized(0)

        def direct(b, _):
            total = taps[0:1] * gz[b, pl.ds(SUB, SUB), :]
            for k in range(1, SUB):
                total = total + taps[k : k + 1] * gz[b, pl.ds(SUB - k, SUB), :]
            local_y[j, b] = total
            return 0

        lax.fori_loop(0, blocks, direct, 0)

    def stage_c(j):
        side, lanes = lane_of(j)
        decay = p_dec[side, :, lanes]
        weight = p_res[side, :, lanes] * jnp.sqrt(2.0 * decay)

        lag_rows = lax.broadcasted_iota(jnp.int32, (SUB, LANES), 0).astype(jnp.float32) + 1.0
        tables = [
            weight[r : r + 1] * jnp.exp(-decay[r : r + 1] * lag_rows) for r in range(ORDER)
        ]
        jump = jnp.exp(decay * (-float(SUB)))
        skip = p_skip[side, :, lanes]
        g = near_slot(j)
        done = 0
        span_fall = jnp.exp(decay * (-float(rows)))
        pltpu.make_async_copy(st_recv.at[j], st_recv.at[j], st_rs.at[j]).wait()

        def gather(i, state):
            return state * span_fall + st_recv[j, me - 1 - i]

        incoming = lax.fori_loop(0, me, gather, jnp.zeros((ORDER, LANES), jnp.float32))
        for b in range(blocks):
            state = local_st[j, b] + incoming
            total = local_y[j, b]
            for r in range(ORDER):
                total = total + tables[r] * state[r : r + 1]
            conv = total.astype(jnp.bfloat16).astype(jnp.float32)
            span = pl.ds(b * SUB, SUB)
            mixed = query_ref[j, span, :] * (conv + skip * gated_ref[j, span, :])
            gobuf[g, span, :] = mixed.astype(jnp.bfloat16)
            incoming = incoming * jump
            if (b + 1) * SUB == sum(gated_cuts[done]):
                i = done

                g_copy(g, i, outward).start()

                @pl.when(is_mid)
                def _():
                    own_copy(i).start()

                done += 1

    tile = 256
    width_out = out_ref.shape[1]

    def project(p, final=False):
        lhs = jnp.concatenate([gobuf[2 * p], gobuf[2 * p + 1]], axis=1)

        def column(t, _):
            cols = pl.ds(pl.multiple_of(t * tile, tile), tile)
            rhs = woutbuf[pl.ds(pl.multiple_of(p * 2 * LANES, 2 * LANES), 2 * LANES), cols]
            part = jnp.dot(lhs, rhs, preferred_element_type=jnp.float32)
            if final:
                out_ref[:, cols] = (acc[:, cols] + part).astype(jnp.bfloat16)
            else:
                acc[:, cols] += part
            return 0

        lax.fori_loop(0, width_out // tile, column, 0)

    def pair_of(half, i):
        return jnp.where(half == 0, i, chunks - 1 - i)

    def recv_gated(g):
        for i in range(len(gated_cuts)):
            g_copy(g, i, outward).wait_recv()

    def relay(g, target):
        for i in range(len(gated_cuts)):
            g_copy(g, i, target).wait_recv()
            g_copy(g, i, target).start()

    @pl.when(is_end)
    def _():
        def lead(j, _):
            a_send[j] = partial(far_slot(j)).astype(jnp.bfloat16)
            for i in range(len(sum_cuts)):
                a_copy(j, i).start()
            return 0

        lax.fori_loop(1, chunks, lead, 0)
        n_send[...] = partial(near_slot(own)).astype(jnp.bfloat16)
        for k in range(depth):
            next_round(k)
        await_own()
        for copy in p_copies:
            copy.wait_recv()
        sq_copy(2, outward).wait_recv()
        set_scale(sq_own[...] + sq_recv[2])
        wout_copy.wait()

        def step(s, _):
            @pl.when(s < own)
            def _():
                total = partial(near_slot(s))
                for i in range(len(sum_cuts)):
                    b_copy(s, i).wait_recv()
                stage_a(s, total + b_recv[s].astype(jnp.float32))

            @pl.when((s >= 1) & (s < own + 1))
            def _():
                stage_b(s - 1)

            @pl.when(s >= 2)
            def _():
                stage_c(s - 2)

            for i in range(len(sum_cuts)):
                @pl.when(s == N_AFTER[i])
                def _():
                    n_copy(i).start()

            @pl.when((s >= 3) & (lax.rem(s, 2) == 1))
            def _():
                project(pair_of(near, (s - 3) // 2))

            return 0

        lax.fori_loop(0, own + 2, step, 0)
        pairs = chunks // 2

        def far_pairs(k, _):
            recv_gated(far_slot(2 * k))
            recv_gated(far_slot(2 * k + 1))
            project(pair_of(1 - near, k))
            return 0

        lax.fori_loop(0, pairs - 2, far_pairs, 0)
        recv_gated(near_slot(own))
        project(pair_of(near, pairs - 1))
        far_pairs(pairs - 2, 0)
        recv_gated(far_slot(own))
        recv_gated(far_slot(own - 1))
        project(pair_of(1 - near, pairs - 1), True)

    @pl.when(is_mid)
    def _():
        def pass_out(s, total):
            for i, (first, size) in enumerate(sum_cuts):
                span = pl.ds(first, size)
                a_copy(s, i).wait_recv()
                theirs = a_recv[s, span, :].astype(jnp.float32)
                a_send[s, span, :] = (total[first : first + size] + theirs).astype(jnp.bfloat16)
                ab_copy(s, i).start()

        def step(s, _):
            total = partial(near_slot(s))
            for i, (first, size) in enumerate(sum_cuts):
                span = pl.ds(first, size)
                b_copy(s, i).wait_recv()
                theirs = b_recv[s, span, :].astype(jnp.float32)
                b_send[s, span, :] = (total[first : first + size] + theirs).astype(jnp.bfloat16)
                b_copy(s, i).start()

            @pl.when(s + 2 < chunks)
            def _():
                pass_out(s + 2, partial(far_slot(s + 2)))

            return 0

        await_own()
        for copy in p_copies:
            copy.start()
        pass_out(0, first_far)
        sq_copy(0, outward).wait_recv()
        sq_send[1] = sq_own[...] + sq_recv[0]
        sq_copy(1, outward).start()
        next_round(0)
        pass_out(1, partial(far_slot(1)))
        sq_copy(1, outward).wait_recv()
        sq_send[2] = sq_own[...] + sq_recv[1]
        sq_copy(2, inward).start()
        set_scale(sq_own[...] + sq_recv[0] + sq_recv[1])
        next_round(1)
        lax.fori_loop(0, own, step, 0)
        for k in range(2, depth):
            next_round(k)
        wout_copy.wait()

        def out(i):
            relay(near_slot(i), outward)

        def back(i):
            relay(far_slot(i), inward)

        out(0)
        total = partial(near_slot(own))
        for i in range(len(sum_cuts)):
            b_copy(own, i).wait_recv()
        for i in range(len(sum_cuts)):
            n_copy(i).wait_recv()
        stage_a(own, total + b_recv[own].astype(jnp.float32) + n_recv[...].astype(jnp.float32))
        out(1)
        stage_b(own)
        back(0)
        out(2)
        project(pair_of(near, 0))
        back(1)
        out(3)
        back(2)
        stage_c(own)
        out(4)
        back(3)
        out(5)
        back(own)
        out(6)
        back(4)
        project(pair_of(near, 1))
        back(5)
        project(pair_of(1 - near, 0))
        back(6)
        project(pair_of(near, 2))
        project(pair_of(near, 3))
        project(pair_of(1 - near, 1))
        project(pair_of(1 - near, 2))
        project(pair_of(1 - near, 3), True)

    def drain(j, _):
        for i in range(len(sum_cuts)):
            a_copy(j, i).wait_send()

        @pl.when(is_mid & (j < own))
        def _():
            for i in range(len(sum_cuts)):
                b_copy(j, i).wait_send()

        @pl.when(is_end & (j < own))
        def _():
            for i in range(len(gated_cuts)):
                g_copy(near_slot(j), i, outward).wait_send()

        @pl.when(is_mid)
        def _():
            for i in range(len(gated_cuts)):
                g_copy(near_slot(j), i, outward).wait_send()

            for i in range(len(gated_cuts)):
                g_copy(far_slot(j), i, inward).wait_send()

        mine = jnp.where(is_end, jnp.where(j < own, 1, 0), jnp.where(j == own, 1, 0))

        @pl.when((mine == 1) & (me < n_ctx - 1))
        def _():
            halo_copy(j).wait_send()

        @pl.when(mine == 1)
        def _():
            pltpu.make_async_copy(st_recv.at[j], st_recv.at[j], st_ss.at[j]).wait()

        return 0

    lax.fori_loop(0, chunks, drain, 0)
    @pl.when(is_end)
    def _():
        for i in range(len(sum_cuts)):
            n_copy(i).wait_send()
        sq_copy(0, outward).wait_send()

    @pl.when(is_mid)
    def _():
        for copy in p_copies:
            copy.wait_send()
        sq_copy(1, outward).wait_send()
        sq_copy(2, inward).wait_send()
        for i in range(len(gated_cuts)):
            own_copy(i).wait_send()


def local(tokens_in, norm_gain, w_qkv, short_filter, residue, decay_rate, skip_bias, w_out):
    rows, feat = tokens_in.shape
    slab = w_qkv.shape[2]
    dev_ch = short_filter.shape[2]
    n_ctx = lax.axis_size("ctx")
    n_ch = lax.axis_size("ch")
    chunks = slab // 2 // LANES
    width = 3 * LANES
    padded = -(-rows // LANES) * LANES
    blocks = rows // SUB
    vmem = pl.BlockSpec(memory_space=pltpu.VMEM)
    hbm = pl.BlockSpec(memory_space=pl.ANY)
    bf, f32 = jnp.bfloat16, jnp.float32
    dma = pltpu.SemaphoreType.DMA
    V = pltpu.VMEM
    n_sum = len(sum_pieces(rows))
    n_gated = len(gated_pieces(rows))
    return pl.pallas_call(
        functools.partial(kernel, n_ctx, n_ch, rows, chunks),
        out_shape=pltpu.VMEM((rows, w_out.shape[1]), bf),
        in_specs=[hbm] * 8,
        out_specs=vmem,
        scratch_shapes=[
            V((rows, feat), bf), V((feat,), bf), V((rows, feat), bf), V((2 * chunks, 3, feat, LANES), bf), V(w_out.shape, bf),
            V((chunks, rows, width), bf), V((chunks, rows, width), bf),
            V((chunks, rows, width), bf), V((chunks, rows, width), bf),
            V((rows, width), bf), V((rows, width), bf),
            V((3, 1, padded), f32), V((3, 1, padded), f32), V((1, padded), f32), V((padded, LANES), f32),
            V((rows, LANES), f32),
            V((2, SHORT, 3, dev_ch), f32), V((2, ORDER, dev_ch), f32), V((2, ORDER, dev_ch), f32),
            V((2, 1, dev_ch), f32),
            V((chunks, 3, HALO + rows, LANES), f32),
            V((chunks, 3, HALO, LANES), bf), V((chunks, 3, HALO, LANES), bf),
            V((chunks, ORDER, LANES), f32), V((chunks, n_ctx - 1, ORDER, LANES), f32),
            V((chunks, blocks, ORDER, LANES), f32), V((blocks, 2 * SUB, LANES), f32),
            V((chunks, rows, LANES), f32), V((chunks, rows, LANES), f32),
            V((chunks, blocks, SUB, LANES), f32), V((2 * chunks, rows, LANES), bf),
            V((rows, w_out.shape[1]), f32),
            dma, dma, dma((4,)), dma((2 * chunks,)), dma, pltpu.SemaphoreType.REGULAR((n_ctx.bit_length() - 1,)),
            dma((chunks, n_sum)), dma((chunks, n_sum)),
            dma((chunks, n_sum)), dma((chunks, n_sum)), dma((n_sum,)), dma((n_sum,)),
            dma((3,)), dma((3,)), dma((4,)), dma((4,)),
            dma((chunks,)), dma((chunks,)), dma((chunks,)), dma((chunks,)),
            dma((2 * chunks, n_gated)), dma((2 * chunks, n_gated)), dma((n_gated,)),
        ],
        compiler_params=pltpu.CompilerParams(
            collective_id=0, has_side_effects=True, vmem_limit_bytes=58 * 2**20
        ),
        name="hyena",
    )(
        tokens_in, norm_gain, jnp.transpose(w_qkv, (1, 0, 2)), short_filter,
        residue.T, decay_rate.T, skip_bias.reshape(1, dev_ch), w_out,
    )


def solution(mesh):
    return jax.shard_map(
        local,
        mesh=mesh,
        in_specs=(
            P("ctx", "ch"),
            P("ch"),
            P("ch", None, None),
            P(None, None, "ch"),
            P("ch", None),
            P("ch", None),
            P("ch"),
            P(None, "ch"),
        ),
        out_specs=P("ctx", "ch"),
        check_vma=False,
    )
```

```python
import functools

import jax
import jax.numpy as jnp
from jax import lax
from jax.experimental import pallas as pl
from jax.experimental.pallas import tpu as pltpu
from jax.sharding import PartitionSpec as P

D = 4096
SHORT = 3
ORDER = 16
LANES = 128
SUB = 32
HALO = 16
N_AFTER = (2, 2)
MESH = pl.DeviceIdType.MESH


def sum_pieces(rows):
    cut = -(-rows // 2 // 32) * 32
    return ((0, cut), (cut, rows - cut))


def gated_pieces(rows):
    cut = -(-rows // 2 // SUB) * SUB
    return ((0, cut), (cut, rows - cut))


def kernel(
    n_ctx, n_ch, rows, chunks,
    tok_hbm, gain_hbm, w_hbm, sf_hbm, res_hbm, dec_hbm, skip_hbm, wout_hbm, out_ref,
    tok, gain, scaled, wbuf, woutbuf, a_send, a_recv, b_send, b_recv, n_send, n_recv,
    sq_send, sq_recv, sq_own, square, scale_ref, p_sf, p_res, p_dec, p_skip,
    fpad, halo_send, halo_recv, st_send, st_recv, local_st, gz, gated_ref, query_ref, local_y, gobuf, acc,
    tok_sem, gain_sem, l_sem, w_sem, wout_sem, rounds, a_ss, a_rs, b_ss, b_rs, n_ss, n_rs, sq_ss, sq_rs, p_ss, p_rs,
    h_ss, h_rs, st_ss, st_rs, g_ss, g_rs, own_ss,
):
    me = lax.axis_index("ctx")
    z = lax.axis_index("ch")
    last = n_ch - 1
    own = chunks - 1
    per = sf_hbm.shape[2] // LANES
    depth = n_ctx.bit_length() - 1
    assert 1 << depth == n_ctx
    blocks = rows // SUB
    sum_cuts = sum_pieces(rows)
    gated_cuts = gated_pieces(rows)
    is_end = (z == 0) | (z == last)
    is_mid = (z > 0) & (z < last)
    near = jnp.where(z * 2 > last, 1, 0)
    step_out = 1 - 2 * near
    outward = jnp.clip(z + step_out, 0, last)
    inward = jnp.clip(z - step_out, 0, last)

    def slot(half, i):
        return jnp.where(half == 0, i, 2 * chunks - 1 - i)

    def near_slot(i):
        return slot(near, i)

    def far_slot(i):
        return slot(1 - near, i)

    def weight_copy(g):
        return pltpu.make_async_copy(
            w_hbm.at[:, :, pl.ds(pl.multiple_of(g * LANES, LANES), LANES)], wbuf.at[g], w_sem.at[g]
        )

    tok_copy = pltpu.make_async_copy(tok_hbm, tok, tok_sem)
    tok_copy.start()
    gain_copy = pltpu.make_async_copy(gain_hbm, gain, gain_sem)
    gain_copy.start()
    weight_copy(far_slot(0)).start()

    def peer(k):
        bit = lax.rem(me // (1 << k), 2)
        return me + (1 << k) * (1 - 2 * bit)

    barrier = pltpu.get_barrier_semaphore()
    pl.semaphore_signal(barrier, inc=1, device_id={"ch": outward}, device_id_type=MESH)

    @pl.when(is_mid)
    def _():
        pl.semaphore_signal(barrier, inc=1, device_id={"ch": inward}, device_id_type=MESH)

    for k in range(depth):
        pl.semaphore_signal(barrier, inc=1, device_id={"ctx": peer(k)}, device_id_type=MESH)

    def call_round(k):
        pl.semaphore_signal(rounds.at[k], inc=1, device_id={"ctx": peer(k)}, device_id_type=MESH)

    def next_round(k):
        pl.semaphore_wait(rounds.at[k], 1)
        if k + 1 < depth:
            call_round(k + 1)

    wout_copy = pltpu.make_async_copy(wout_hbm, woutbuf, wout_sem)
    home = jnp.where(is_end, 0, 1)
    l_copies = [
        pltpu.make_async_copy(src, dst.at[home], l_sem.at[i])
        for i, (src, dst) in enumerate(
            ((sf_hbm, p_sf), (res_hbm, p_res), (dec_hbm, p_dec), (skip_hbm, p_skip))
        )
    ]
    tok_copy.wait()
    gain_copy.wait()
    wide = tok[...].astype(jnp.float32)
    scaled[...] = (wide * gain[...].astype(jnp.float32).reshape(1, -1)).astype(jnp.bfloat16)

    def partial(g):
        weight_copy(g).wait()
        taps = jnp.concatenate([wbuf[g, s] for s in range(3)], axis=1)
        return jnp.dot(scaled[...], taps, preferred_element_type=jnp.float32)

    def a_copy(j, i):
        first, size = sum_cuts[i]
        return pltpu.make_async_remote_copy(
            src_ref=a_send.at[j, pl.ds(first, size)], dst_ref=a_recv.at[j, pl.ds(first, size)],
            send_sem=a_ss.at[j, i], recv_sem=a_rs.at[j, i],
            device_id={"ch": outward}, device_id_type=MESH,
        )

    def ab_copy(j, i):
        first, size = sum_cuts[i]
        return pltpu.make_async_remote_copy(
            src_ref=a_send.at[j, pl.ds(first, size)], dst_ref=b_recv.at[j, pl.ds(first, size)],
            send_sem=a_ss.at[j, i], recv_sem=b_rs.at[j, i],
            device_id={"ch": outward}, device_id_type=MESH,
        )

    def b_copy(j, i):
        first, size = sum_cuts[i]
        return pltpu.make_async_remote_copy(
            src_ref=b_send.at[j, pl.ds(first, size)], dst_ref=b_recv.at[j, pl.ds(first, size)],
            send_sem=b_ss.at[j, i], recv_sem=b_rs.at[j, i],
            device_id={"ch": inward}, device_id_type=MESH,
        )

    def n_copy(i):
        first, size = sum_cuts[i]
        return pltpu.make_async_remote_copy(
            src_ref=n_send.at[pl.ds(first, size)], dst_ref=n_recv.at[pl.ds(first, size)],
            send_sem=n_ss.at[i], recv_sem=n_rs.at[i],
            device_id={"ch": outward}, device_id_type=MESH,
        )

    def sq_copy(way, target):
        return pltpu.make_async_remote_copy(
            src_ref=sq_send.at[way], dst_ref=sq_recv.at[way], send_sem=sq_ss.at[way],
            recv_sem=sq_rs.at[way], device_id={"ch": target}, device_id_type=MESH,
        )

    p_copies = [
        pltpu.make_async_remote_copy(
            src_ref=dst.at[1], dst_ref=dst.at[1], send_sem=p_ss.at[i], recv_sem=p_rs.at[i],
            device_id={"ch": inward}, device_id_type=MESH,
        )
        for i, dst in enumerate((p_sf, p_res, p_dec, p_skip))
    ]

    def halo_copy(j):
        return pltpu.make_async_remote_copy(
            src_ref=halo_send.at[j], dst_ref=halo_recv.at[j], send_sem=h_ss.at[j],
            recv_sem=h_rs.at[j], device_id={"ctx": jnp.minimum(me + 1, n_ctx - 1)}, device_id_type=MESH,
        )

    def state_copy(j, k):
        return pltpu.make_async_remote_copy(
            src_ref=st_send.at[j], dst_ref=st_recv.at[j, k - 1], send_sem=st_ss.at[j],
            recv_sem=st_rs.at[j], device_id={"ctx": lax.rem(me + k, n_ctx)}, device_id_type=MESH,
        )

    def g_copy(g, i, target):
        first, size = gated_cuts[i]
        piece = gobuf.at[g, pl.ds(first, size)]
        return pltpu.make_async_remote_copy(
            src_ref=piece, dst_ref=piece, send_sem=g_ss.at[g, i], recv_sem=g_rs.at[g, i],
            device_id={"ch": target}, device_id_type=MESH,
        )

    def far_end_copy(g, i):
        first, size = gated_cuts[i]
        piece = gobuf.at[g, pl.ds(first, size)]
        return pltpu.make_async_remote_copy(
            src_ref=piece, dst_ref=piece, send_sem=own_ss.at[i], recv_sem=g_rs.at[g, i],
            device_id={"ch": last - z}, device_id_type=MESH,
        )

    def own_copy(i):
        first, size = gated_cuts[i]
        piece = gobuf.at[near_slot(own), pl.ds(first, size)]
        return pltpu.make_async_remote_copy(
            src_ref=piece, dst_ref=piece, send_sem=own_ss.at[i], recv_sem=g_rs.at[near_slot(own), i],
            device_id={"ch": inward}, device_id_type=MESH,
        )

    first_far = partial(far_slot(0))
    a_send[0] = first_far.astype(jnp.bfloat16)

    @pl.when(is_end)
    def _():
        pl.semaphore_wait(barrier, 1 + depth)
        a_copy(0, 0).start()

    @pl.when(is_mid)
    def _():
        pl.semaphore_wait(barrier, 2 + depth)

    call_round(0)
    for copy in l_copies:
        copy.start()
    weight_copy(near_slot(0)).start()

    def start_weights(j, _):
        weight_copy(far_slot(j)).start()
        weight_copy(near_slot(j)).start()
        return 0

    lax.fori_loop(1, chunks, start_weights, 0)
    wout_copy.start()
    again = tok[...].astype(jnp.float32)
    again = again * again
    folded = again[:, :LANES]
    for k in range(1, again.shape[1] // LANES):
        folded = folded + again[:, k * LANES : (k + 1) * LANES]
    square[...] = jnp.zeros_like(square)
    square[pl.ds(0, rows), :] = folded
    sq_own[...] = jnp.sum(square[...].T, axis=0, keepdims=True)

    @pl.when(is_end)
    def _():
        sq_send[0] = sq_own[...]
        sq_copy(0, outward).start()
        for i in range(1, len(sum_cuts)):
            a_copy(0, i).start()

    def await_own():
        for copy in l_copies:
            copy.wait()

    gz[...] = jnp.zeros_like(gz)
    acc[...] = jnp.zeros_like(acc)

    def set_scale(total):
        mean_sq = jnp.broadcast_to(total * (1.0 / D), (LANES, total.shape[1])).T
        scale_ref[...] = lax.rsqrt(mean_sq + 1e-06)[:rows]

    def stage_a(j, proj):
        scale = scale_ref[...]
        for s in range(3):
            tail = proj[rows - HALO :, s * LANES : (s + 1) * LANES] * scale[rows - HALO :]
            halo_send[j, s] = tail.astype(jnp.bfloat16)

        @pl.when(me < n_ctx - 1)
        def _():
            halo_copy(j).start()

        for s in range(3):
            feats = (proj[:, s * LANES : (s + 1) * LANES] * scale).astype(jnp.bfloat16)
            fpad[j, s, pl.ds(HALO, rows), :] = feats.astype(jnp.float32)

    def lane_of(j):
        place = lax.rem(j, per)
        place = jnp.where(near == 0, place, per - 1 - place)
        return j // per, pl.ds(pl.multiple_of(place * LANES, LANES), LANES)

    def stage_b(j):
        side, lanes = lane_of(j)
        decay = p_dec[side, :, lanes]
        weight = p_res[side, :, lanes] * jnp.sqrt(2.0 * decay)
        lag_rows = lax.broadcasted_iota(jnp.int32, (SUB, LANES), 0).astype(jnp.float32)
        taps = jnp.zeros((SUB, LANES), jnp.float32)
        for r in range(ORDER):
            taps = taps + weight[r : r + 1] * jnp.exp(-decay[r : r + 1] * lag_rows)
        falls = [jnp.exp(decay * (-float(SUB - 1 - u))) for u in range(SUB)]
        jump = jnp.exp(decay * (-float(SUB)))

        @pl.when(me > 0)
        def _():
            halo_copy(j).wait_recv()
            for s in range(3):
                fpad[j, s, pl.ds(0, HALO), :] = halo_recv[j, s].astype(jnp.float32)

        @pl.when(me == 0)
        def _():
            for s in range(3):
                fpad[j, s, pl.ds(0, HALO), :] = jnp.zeros((HALO, LANES), jnp.float32)

        def featurized(s):
            total = p_sf[side, 0, pl.ds(s, 1), lanes] * fpad[j, s, pl.ds(HALO, rows), :]
            for lag in range(1, SHORT):
                tap = p_sf[side, lag, pl.ds(s, 1), lanes]
                total = total + tap * fpad[j, s, pl.ds(HALO - lag, rows), :]
            return total

        gated = (featurized(1) * featurized(2)).astype(jnp.bfloat16).astype(jnp.float32)
        gated_ref[j] = gated
        for b in range(blocks):
            gz[b, pl.ds(SUB, SUB), :] = gated[b * SUB : (b + 1) * SUB]

        def block(b, state):
            local_st[j, b] = state
            parts = [state * jump] + [None] * 3
            for u in range(SUB):
                term = falls[u] * gz[b, pl.ds(SUB + u, 1), :]
                way = (u + 1) % 4
                parts[way] = term if parts[way] is None else parts[way] + term
            return (parts[0] + parts[1]) + (parts[2] + parts[3])

        state = lax.fori_loop(0, blocks, block, jnp.zeros((ORDER, LANES), jnp.float32))
        st_send[j] = state

        if n_ctx <= 8:
            for k in range(1, n_ctx):
                state_copy(j, k).start()
        else:
            lax.fori_loop(1, n_ctx, lambda k, _: (state_copy(j, k).start(), 0)[1], 0)

        query_ref[j] = featurized(0)

        def direct(b, _):
            total = taps[0:1] * gz[b, pl.ds(SUB, SUB), :]
            for k in range(1, SUB):
                total = total + taps[k : k + 1] * gz[b, pl.ds(SUB - k, SUB), :]
            local_y[j, b] = total
            return 0

        lax.fori_loop(0, blocks, direct, 0)

    def stage_c(j):
        side, lanes = lane_of(j)
        decay = p_dec[side, :, lanes]
        weight = p_res[side, :, lanes] * jnp.sqrt(2.0 * decay)

        lag_rows = lax.broadcasted_iota(jnp.int32, (SUB, LANES), 0).astype(jnp.float32) + 1.0
        tables = [
            weight[r : r + 1] * jnp.exp(-decay[r : r + 1] * lag_rows) for r in range(ORDER)
        ]
        jump = jnp.exp(decay * (-float(SUB)))
        skip = p_skip[side, :, lanes]
        g = near_slot(j)
        done = 0
        span_fall = jnp.exp(decay * (-float(rows)))
        pltpu.make_async_copy(st_recv.at[j], st_recv.at[j], st_rs.at[j]).wait()

        def gather(i, state):
            return state * span_fall + st_recv[j, me - 1 - i]

        incoming = lax.fori_loop(0, me, gather, jnp.zeros((ORDER, LANES), jnp.float32))
        for b in range(blocks):
            state = local_st[j, b] + incoming
            total = local_y[j, b]
            for r in range(ORDER):
                total = total + tables[r] * state[r : r + 1]
            conv = total.astype(jnp.bfloat16).astype(jnp.float32)
            span = pl.ds(b * SUB, SUB)
            mixed = query_ref[j, span, :] * (conv + skip * gated_ref[j, span, :])
            gobuf[g, span, :] = mixed.astype(jnp.bfloat16)
            incoming = incoming * jump
            if (b + 1) * SUB == sum(gated_cuts[done]):
                i = done

                g_copy(g, i, outward).start()

                @pl.when(is_mid)
                def _():
                    own_copy(i).start()

                done += 1

    tile = 256
    width_out = out_ref.shape[1]

    def project(p, final=False):
        lhs = jnp.concatenate([gobuf[2 * p], gobuf[2 * p + 1]], axis=1)

        def column(t, _):
            cols = pl.ds(pl.multiple_of(t * tile, tile), tile)
            rhs = woutbuf[pl.ds(pl.multiple_of(p * 2 * LANES, 2 * LANES), 2 * LANES), cols]
            part = jnp.dot(lhs, rhs, preferred_element_type=jnp.float32)
            if final:
                out_ref[:, cols] = (acc[:, cols] + part).astype(jnp.bfloat16)
            else:
                acc[:, cols] += part
            return 0

        lax.fori_loop(0, width_out // tile, column, 0)

    def pair_of(half, i):
        return jnp.where(half == 0, i, chunks - 1 - i)

    def recv_gated(g):
        for i in range(len(gated_cuts)):
            g_copy(g, i, outward).wait_recv()

    def relay(g, target):
        for i in range(len(gated_cuts)):
            g_copy(g, i, target).wait_recv()
            g_copy(g, i, target).start()

    @pl.when(is_end)
    def _():
        def lead(j, _):
            a_send[j] = partial(far_slot(j)).astype(jnp.bfloat16)
            for i in range(len(sum_cuts)):
                a_copy(j, i).start()
            return 0

        lax.fori_loop(1, chunks, lead, 0)
        n_send[...] = partial(near_slot(own)).astype(jnp.bfloat16)
        for k in range(depth):
            next_round(k)
        await_own()
        for copy in p_copies:
            copy.wait_recv()
        sq_copy(2, outward).wait_recv()
        set_scale(sq_own[...] + sq_recv[2])
        wout_copy.wait()

        def step(s, _):
            @pl.when(s < own)
            def _():
                total = partial(near_slot(s))
                for i in range(len(sum_cuts)):
                    b_copy(s, i).wait_recv()
                stage_a(s, total + b_recv[s].astype(jnp.float32))

            @pl.when((s >= 1) & (s < own + 1))
            def _():
                stage_b(s - 1)

            @pl.when(s >= 2)
            def _():
                stage_c(s - 2)

            for i in range(len(sum_cuts)):
                @pl.when(s == N_AFTER[i])
                def _():
                    n_copy(i).start()

            @pl.when((s >= 3) & (lax.rem(s, 2) == 1))
            def _():
                project(pair_of(near, (s - 3) // 2))

            return 0

        lax.fori_loop(0, own + 2, step, 0)
        pairs = chunks // 2

        def far_pairs(k, _):
            recv_gated(far_slot(2 * k))
            recv_gated(far_slot(2 * k + 1))
            project(pair_of(1 - near, k))
            return 0

        lax.fori_loop(0, pairs - 2, far_pairs, 0)
        recv_gated(near_slot(own))
        project(pair_of(near, pairs - 1))
        far_pairs(pairs - 2, 0)
        recv_gated(far_slot(own))
        recv_gated(far_slot(own - 1))
        project(pair_of(1 - near, pairs - 1), True)

    @pl.when(is_mid)
    def _():
        def pass_out(s, total):
            for i, (first, size) in enumerate(sum_cuts):
                span = pl.ds(first, size)
                a_copy(s, i).wait_recv()
                theirs = a_recv[s, span, :].astype(jnp.float32)
                a_send[s, span, :] = (total[first : first + size] + theirs).astype(jnp.bfloat16)
                ab_copy(s, i).start()

        def step(s, _):
            total = partial(near_slot(s))
            for i, (first, size) in enumerate(sum_cuts):
                span = pl.ds(first, size)
                b_copy(s, i).wait_recv()
                theirs = b_recv[s, span, :].astype(jnp.float32)
                b_send[s, span, :] = (total[first : first + size] + theirs).astype(jnp.bfloat16)
                b_copy(s, i).start()

            @pl.when(s + 2 < chunks)
            def _():
                pass_out(s + 2, partial(far_slot(s + 2)))

            return 0

        await_own()
        for copy in p_copies:
            copy.start()
        pass_out(0, first_far)
        sq_copy(0, outward).wait_recv()
        sq_send[1] = sq_own[...] + sq_recv[0]
        sq_copy(1, outward).start()
        next_round(0)
        pass_out(1, partial(far_slot(1)))
        sq_copy(1, outward).wait_recv()
        sq_send[2] = sq_own[...] + sq_recv[1]
        sq_copy(2, inward).start()
        set_scale(sq_own[...] + sq_recv[0] + sq_recv[1])
        next_round(1)
        lax.fori_loop(0, own, step, 0)
        for k in range(2, depth):
            next_round(k)
        wout_copy.wait()

        def out(i):
            relay(near_slot(i), outward)

        def back(i):
            relay(far_slot(i), inward)

        out(0)
        total = partial(near_slot(own))
        for i in range(len(sum_cuts)):
            b_copy(own, i).wait_recv()
        for i in range(len(sum_cuts)):
            n_copy(i).wait_recv()
        stage_a(own, total + b_recv[own].astype(jnp.float32) + n_recv[...].astype(jnp.float32))
        out(1)
        stage_b(own)
        back(0)
        out(2)
        project(pair_of(near, 0))
        back(1)
        out(3)
        back(2)
        stage_c(own)
        out(4)
        back(3)
        out(5)
        back(own)
        out(6)
        back(4)
        back(5)
        back(6)
        project(pair_of(near, 1))
        project(pair_of(1 - near, 0))
        project(pair_of(near, 2))
        project(pair_of(near, 3))
        project(pair_of(1 - near, 1))
        project(pair_of(1 - near, 2))
        project(pair_of(1 - near, 3), True)

    def drain(j, _):
        for i in range(len(sum_cuts)):
            a_copy(j, i).wait_send()

        @pl.when(is_mid & (j < own))
        def _():
            for i in range(len(sum_cuts)):
                b_copy(j, i).wait_send()

        @pl.when(is_end & (j < own))
        def _():
            for i in range(len(gated_cuts)):
                g_copy(near_slot(j), i, outward).wait_send()

        @pl.when(is_mid)
        def _():
            for i in range(len(gated_cuts)):
                g_copy(near_slot(j), i, outward).wait_send()

            for i in range(len(gated_cuts)):
                g_copy(far_slot(j), i, inward).wait_send()

        mine = jnp.where(is_end, jnp.where(j < own, 1, 0), jnp.where(j == own, 1, 0))

        @pl.when((mine == 1) & (me < n_ctx - 1))
        def _():
            halo_copy(j).wait_send()

        @pl.when(mine == 1)
        def _():
            pltpu.make_async_copy(st_recv.at[j], st_recv.at[j], st_ss.at[j]).wait()

        return 0

    lax.fori_loop(0, chunks, drain, 0)
    @pl.when(is_end)
    def _():
        for i in range(len(sum_cuts)):
            n_copy(i).wait_send()
        sq_copy(0, outward).wait_send()

    @pl.when(is_mid)
    def _():
        for copy in p_copies:
            copy.wait_send()
        sq_copy(1, outward).wait_send()
        sq_copy(2, inward).wait_send()
        for i in range(len(gated_cuts)):
            own_copy(i).wait_send()


def local(tokens_in, norm_gain, w_qkv, short_filter, residue, decay_rate, skip_bias, w_out):
    rows, feat = tokens_in.shape
    slab = w_qkv.shape[2]
    dev_ch = short_filter.shape[2]
    n_ctx = lax.axis_size("ctx")
    n_ch = lax.axis_size("ch")
    chunks = slab // 2 // LANES
    width = 3 * LANES
    padded = -(-rows // LANES) * LANES
    blocks = rows // SUB
    vmem = pl.BlockSpec(memory_space=pltpu.VMEM)
    hbm = pl.BlockSpec(memory_space=pl.ANY)
    bf, f32 = jnp.bfloat16, jnp.float32
    dma = pltpu.SemaphoreType.DMA
    V = pltpu.VMEM
    n_sum = len(sum_pieces(rows))
    n_gated = len(gated_pieces(rows))
    return pl.pallas_call(
        functools.partial(kernel, n_ctx, n_ch, rows, chunks),
        out_shape=pltpu.VMEM((rows, w_out.shape[1]), bf),
        in_specs=[hbm] * 8,
        out_specs=vmem,
        scratch_shapes=[
            V((rows, feat), bf), V((feat,), bf), V((rows, feat), bf), V((2 * chunks, 3, feat, LANES), bf), V(w_out.shape, bf),
            V((chunks, rows, width), bf), V((chunks, rows, width), bf),
            V((chunks, rows, width), bf), V((chunks, rows, width), bf),
            V((rows, width), bf), V((rows, width), bf),
            V((3, 1, padded), f32), V((3, 1, padded), f32), V((1, padded), f32), V((padded, LANES), f32),
            V((rows, LANES), f32),
            V((2, SHORT, 3, dev_ch), f32), V((2, ORDER, dev_ch), f32), V((2, ORDER, dev_ch), f32),
            V((2, 1, dev_ch), f32),
            V((chunks, 3, HALO + rows, LANES), f32),
            V((chunks, 3, HALO, LANES), bf), V((chunks, 3, HALO, LANES), bf),
            V((chunks, ORDER, LANES), f32), V((chunks, n_ctx - 1, ORDER, LANES), f32),
            V((chunks, blocks, ORDER, LANES), f32), V((blocks, 2 * SUB, LANES), f32),
            V((chunks, rows, LANES), f32), V((chunks, rows, LANES), f32),
            V((chunks, blocks, SUB, LANES), f32), V((2 * chunks, rows, LANES), bf),
            V((rows, w_out.shape[1]), f32),
            dma, dma, dma((4,)), dma((2 * chunks,)), dma, pltpu.SemaphoreType.REGULAR((n_ctx.bit_length() - 1,)),
            dma((chunks, n_sum)), dma((chunks, n_sum)),
            dma((chunks, n_sum)), dma((chunks, n_sum)), dma((n_sum,)), dma((n_sum,)),
            dma((3,)), dma((3,)), dma((4,)), dma((4,)),
            dma((chunks,)), dma((chunks,)), dma((chunks,)), dma((chunks,)),
            dma((2 * chunks, n_gated)), dma((2 * chunks, n_gated)), dma((n_gated,)),
        ],
        compiler_params=pltpu.CompilerParams(
            collective_id=0, has_side_effects=True, vmem_limit_bytes=58 * 2**20
        ),
        name="hyena",
    )(
        tokens_in, norm_gain, jnp.transpose(w_qkv, (1, 0, 2)), short_filter,
        residue.T, decay_rate.T, skip_bias.reshape(1, dev_ch), w_out,
    )


def solution(mesh):
    return jax.shard_map(
        local,
        mesh=mesh,
        in_specs=(
            P("ctx", "ch"),
            P("ch"),
            P("ch", None, None),
            P(None, None, "ch"),
            P("ch", None),
            P("ch", None),
            P("ch"),
            P(None, "ch"),
        ),
        out_specs=P("ctx", "ch"),
        check_vma=False,
    )
```
